512 devices in a mesh: tensor: 8 (over z_hi, core), ctx: 64 (over x, z_lo, y).
Axes of the slice: x: 4, y: 8, z: 8 (z_hi: 4, z_lo: 2; z = z_hi * 2 + z_lo), core: 2. Of those that a mesh axis runs over, the one named last changes fastest.
Arguments:
- queries: bfloat16 [1024, 3072], P('ctx', 'tensor'), may hold values from -12 to 12
- key_cache: bfloat16 [128, 512, 3072], P('ctx', None, 'tensor'), may hold values from -12 to 12
- value_cache: bfloat16 [128, 512, 3072], P('ctx', None, 'tensor'), may hold values from -6 to 6
- cached_len: int32 [4], replicated, may hold values from 3968 to 7936, as said below
- block_slot: int32 [4, 16], replicated, may hold values from -1 to 127, as said below
- out_weight: bfloat16 [3072, 3072], P('tensor', 'ctx'), may hold values from -3 to 3
- norm_gain: float32 [3072], P('tensor'), may hold values from 0.5 to 1.5
Outputs:
- normed: bfloat16 [1024, 3072], P('ctx', 'tensor')
The draws below stay inside these ranges and needn't reach their ends.
Inputs may be any that keep to these rules, and one draw needn't show every extreme that they name: `cached_len`: one request has exactly 7936 cached tokens. `block_slot`: entry [r, b] is a slot number (device index along ctx times 2 plus the slot on that device) for b below ceil((cached_len[r] + 256) / 512), and -1 beyond; no slot is named twice; the 2 slots of some device are all named.
All inputs are finite; a program needn't handle non-finite values.
Results may differ from the reference program's by a relative error of at most 0.018.
Values may be sent and summed in bfloat16 or wider, within the bound.
A program may use at most 64 MiB of HBM per device.

```python
import math
import jax
import jax.numpy as jnp
from jax import lax

D = 3072
HEADS = 32
HD = 96
REQS = 4
BLOCK = 512
SPAN = 256
SLOTS = 2
MAXB = 16
CACHED_MAX = 7936
CACHED_MIN = 3968
TOK = 1024
N_CTX = 64


def layout(key):
    base = jax.random.fold_in(key, 11)
    key_len, key_top, key_dev, key_order = jax.random.split(base, 4)
    lengths = jax.random.randint(key_len, (REQS,), CACHED_MIN, CACHED_MAX + 1, dtype=jnp.int32)
    longest = jax.random.randint(key_top, (), 0, REQS, dtype=jnp.int32)
    lengths = jnp.where(jnp.arange(REQS, dtype=jnp.int32) == longest, CACHED_MAX, lengths).astype(jnp.int32)
    needed = (lengths + SPAN + BLOCK - 1) // BLOCK
    capacity = N_CTX * SLOTS
    slot_ids = jnp.arange(capacity, dtype=jnp.int32)
    filled = jax.random.randint(key_dev, (), 0, N_CTX, dtype=jnp.int32)
    ranking = jax.random.randint(key_order, (capacity,), 0, capacity, dtype=jnp.int32) * capacity + slot_ids
    ranking = jnp.where(slot_ids // SLOTS == filled, slot_ids % SLOTS - SLOTS, ranking)
    sequence = jnp.argsort(ranking).astype(jnp.int32)
    starts = jnp.cumsum(needed) - needed
    entries = jnp.arange(MAXB, dtype=jnp.int32)
    position = jnp.minimum(starts[:, None] + entries[None, :], capacity - 1)
    table = jnp.where(entries[None, :] < needed[:, None], sequence[position], -1)
    return (lengths, table.astype(jnp.int32))


def draw_cached_len(key, part):
    return layout(key)[0]


def draw_block_slot(key, part):
    return layout(key)[1]


def draw_queries(key, part):
    key_main = jax.random.fold_in(key, 31)
    values = jnp.clip(jax.random.normal(key_main, (TOK, HEADS * HD), jnp.float32), -6.0, 6.0)
    return values.astype(jnp.bfloat16)


def draw_key_cache(key, part):
    key_main = jax.random.fold_in(key, 41)
    capacity = N_CTX * SLOTS
    values = jnp.clip(jax.random.normal(key_main, (capacity, BLOCK, HEADS * HD), jnp.float32), -6.0, 6.0)
    return values.astype(jnp.bfloat16)


def draw_out_weight(key, part):
    key_main = jax.random.fold_in(key, 51)
    key_col = jax.random.fold_in(key, 53)
    columns = jnp.arange(D, dtype=jnp.float32) / D
    spread = jnp.exp(math.log(10.0) * jax.random.uniform(key_col, (D,), jnp.float32))
    rising = jnp.exp(math.log(3.0) * columns)
    base = jnp.clip(jax.random.normal(key_main, (HEADS * HD, D), jnp.float32), -5.0, 5.0)
    values = base * (spread * rising)[None, :] / math.sqrt(HEADS * HD)
    return jnp.clip(values, -3.0, 3.0).astype(jnp.bfloat16)


def block_scale(stream_key, dims, cuts, least, high):
    factor_of, own = 1.0, jax.random.fold_in(stream_key, 6)
    for axis_at, parts in cuts:
        draws = jnp.exp(jax.random.uniform(jax.random.fold_in(own, axis_at), (parts,), jnp.float32, least / len(cuts), high / len(cuts)))
        factor_of = factor_of * jnp.repeat(draws, dims[axis_at] // parts).reshape([-1 if axis == axis_at else 1 for axis in range(len(dims))])
    return factor_of


def noise(own_key, shape, scale, reach, pieces=(), kind=jnp.bfloat16):
    values = scale * jax.random.normal(own_key, shape, jnp.float32)
    if pieces:
        values = values * block_scale(own_key, shape, pieces, -0.22, 0.18)
    return jnp.clip(values, -reach, reach).astype(kind)


def setup_inputs(seed: int = 0) -> dict:
    streams_of = jax.random.split(jax.random.key(seed), 8)
    return {
        "queries": draw_queries(jax.random.fold_in(streams_of[7], 71), 0),
        "key_cache": draw_key_cache(jax.random.fold_in(streams_of[7], 71), 0),
        "value_cache": noise(streams_of[2], (N_CTX * SLOTS, BLOCK, HEADS * HD), 1.0, 6.0, ((0, 64), (2, 8))),
        "cached_len": draw_cached_len(jax.random.fold_in(streams_of[7], 71), 0),
        "block_slot": draw_block_slot(jax.random.fold_in(streams_of[7], 71), 0),
        "out_weight": draw_out_weight(jax.random.fold_in(streams_of[7], 71), 0),
        "norm_gain": jnp.clip(1.0 + 0.1 * jax.random.normal(streams_of[6], (D,), jnp.float32), 0.5, 1.5),
    }


def request_attention(query_rows, key_rows, value_rows, start):
    query_pos = start + jnp.arange(SPAN, dtype=jnp.int32)
    key_pos = jnp.arange(MAXB * BLOCK, dtype=jnp.int32)
    visible = key_pos[None, :] <= query_pos[:, None]

    def one_head(head):
        query_head = lax.dynamic_slice_in_dim(query_rows, head * HD, HD, 1)
        key_head = lax.dynamic_slice_in_dim(key_rows, head * HD, HD, 1)
        value_head = lax.dynamic_slice_in_dim(value_rows, head * HD, HD, 1)
        scores = jnp.dot(query_head, key_head.T, preferred_element_type=jnp.float32) * (1.0 / math.sqrt(HD))
        highest = lax.optimization_barrier(jnp.max(jnp.where(visible, scores, -1e+30), axis=1, keepdims=True))
        weights = jnp.where(visible, jnp.exp(scores - highest), 0.0)
        totals = lax.optimization_barrier(jnp.sum(weights, axis=1, keepdims=True))
        mixed = jnp.dot(weights.astype(jnp.bfloat16), value_head, preferred_element_type=jnp.float32)
        return mixed / totals
    per_head = lax.map(one_head, jnp.arange(HEADS, dtype=jnp.int32))
    return jnp.transpose(per_head, (1, 0, 2)).reshape(SPAN, HEADS * HD)

def reference(queries, key_cache, value_cache, cached_len, block_slot, out_weight, norm_gain):

    def one_request(request):
        slot_rows = jnp.maximum(block_slot[request], 0).astype(jnp.int32)
        key_rows = key_cache[slot_rows].reshape(MAXB * BLOCK, HEADS * HD)
        value_rows = value_cache[slot_rows].reshape(MAXB * BLOCK, HEADS * HD)
        query_rows = lax.dynamic_slice_in_dim(queries, (request * SPAN).astype(jnp.int32), SPAN, 0)
        return request_attention(query_rows, key_rows, value_rows, cached_len[request])
    attn = lax.map(one_request, jnp.arange(REQS, dtype=jnp.int32))
    attn = attn.reshape(REQS * SPAN, HEADS * HD).astype(jnp.bfloat16)
    proj = jnp.dot(attn, out_weight, preferred_element_type=jnp.float32)
    mean_square = lax.optimization_barrier(jnp.mean(proj * proj, axis=1, keepdims=True))
    return (proj * lax.rsqrt(mean_square + 1e-05) * norm_gain[None, :]).astype(jnp.bfloat16)
```

```python
import functools
import math

import jax
import jax.numpy as jnp
from jax import lax
from jax.experimental import pallas as pl
from jax.experimental.pallas import tpu as pltpu
from jax.sharding import PartitionSpec as P

HD = 96
REQS = 4
HEADS_DEV = 4
FEATS = 384
SPAN = 256
PLANE = 16
ROWS = 16
YS = 8
GROUPS = 8
D = 3072
NEG = -1e30
WIDE = FEATS + 128


def remote(src, dst, send, recv, device):
    return pltpu.make_async_remote_copy(
        src_ref=src,
        dst_ref=dst,
        send_sem=send,
        recv_sem=recv,
        device_id=device,
        device_id_type=pl.DeviceIdType.MESH,
    )


def signal(sem, device):
    pl.semaphore_signal(sem, inc=1, device_id=device, device_id_type=pl.DeviceIdType.MESH)


def gather_kernel(q_ref, out_ref, own_sem, send_plane, send_x, recv):
    me = lax.axis_index("ctx")
    x, j = me // PLANE, me % PLANE
    barrier = pltpu.get_barrier_semaphore()

    def greet(k, c):
        signal(barrier, {"ctx": x * PLANE + (j + k) % PLANE})
        return c

    lax.fori_loop(1, PLANE, greet, 0)
    for dx in range(1, REQS):
        signal(barrier, {"ctx": (x + dx) % REQS * PLANE + j})
    own = pltpu.make_async_copy(q_ref, out_ref.at[me], own_sem)
    own.start()
    pl.semaphore_wait(barrier, PLANE - 1 + REQS - 1)

    def to_plane(k):
        there = x * PLANE + (j + k) % PLANE
        return remote(q_ref, out_ref.at[me], send_plane.at[k], recv.at[me], {"ctx": there})

    def to_x(k, dx):
        block = x * PLANE + (j + PLANE - k) % PLANE
        there = (x + dx) % REQS * PLANE + j
        src = q_ref if isinstance(k, int) and k == 0 else out_ref.at[block]
        return remote(
            src, out_ref.at[block], send_x.at[dx - 1, k], recv.at[block], {"ctx": there}
        )

    def start_plane(k, c):
        to_plane(k).start()
        return c

    for dx in range(1, REQS):
        to_x(0, dx).start()
    lax.fori_loop(1, PLANE, start_plane, 0)

    def forward(k, c):
        block = x * PLANE + (j + PLANE - k) % PLANE
        pltpu.make_async_copy(out_ref.at[block], out_ref.at[block], recv.at[block]).wait()
        for dx in range(1, REQS):
            to_x(k, dx).start()
        return c

    lax.fori_loop(1, PLANE, forward, 0)

    def arrive(k, c):
        for dx in range(1, REQS):
            block = (x + dx) % REQS * PLANE + (j + PLANE - k) % PLANE
            pltpu.make_async_copy(out_ref.at[block], out_ref.at[block], recv.at[block]).wait()
        return c

    lax.fori_loop(0, PLANE, arrive, 0)

    def sent(k, c):
        to_plane(k).wait_send()
        for dx in range(1, REQS):
            to_x(k, dx).wait_send()
        return c

    lax.fori_loop(1, PLANE, sent, 0)
    for dx in range(1, REQS):
        to_x(0, dx).wait_send()
    own.wait()


def split_parts(lse):
    lane = lax.broadcasted_iota(jnp.int32, lse.shape, 1)
    high = lse.astype(jnp.bfloat16).astype(jnp.float32)
    rest = lse - high
    mid = rest.astype(jnp.bfloat16).astype(jnp.float32)
    low = rest - mid
    part = lane % 4
    picked = jnp.where(part == 0, high, jnp.where(part == 1, mid, jnp.where(part == 2, low, 0.0)))
    return jnp.where(lane < 4 * HEADS_DEV, picked, 0.0).astype(jnp.bfloat16)


def attention_kernel(table_ref, len_ref, q_ref, k_ref, v_ref, out_ref):
    slots = k_ref.shape[0]
    block_rows = k_ref.shape[1]
    me = lax.axis_index("ctx")
    scale = 1.0 / math.sqrt(HD)
    empty_parts = split_parts(jnp.full((SPAN, 128), NEG, jnp.float32))
    for r in range(REQS):
        out_ref[r, :, :FEATS] = jnp.zeros((SPAN, FEATS), jnp.bfloat16)
        out_ref[r, :, FEATS:] = empty_parts
    before = None
    for s in range(slots):
        slot_id = me * slots + s
        found = jnp.int32(-1)
        for r in range(REQS):
            for b in range(table_ref.shape[1]):
                found = jnp.where(table_ref[r, b] == slot_id, r * 16 + b, found)
        used = found >= 0
        request = jnp.where(used, found // 16, 0)
        first_key = jnp.where(used, found % 16 * block_rows, 1 << 28)
        diff = (
            lax.broadcasted_iota(jnp.int32, (SPAN, block_rows), 1)
            - lax.broadcasted_iota(jnp.int32, (SPAN, block_rows), 0)
        )
        visible = diff <= len_ref[request] - first_key
        query = q_ref[pl.ds(pl.multiple_of(request * SPAN, SPAN), SPAN), :]
        tiles = [jnp.zeros((SPAN, 128), jnp.float32) for _ in range(FEATS // 128)]
        lane = lax.broadcasted_iota(jnp.int32, (SPAN, 128), 1)
        lse = jnp.full((SPAN, 128), NEG, jnp.float32)
        for h in range(HEADS_DEV):
            first, last = h * HD // 128, (h * HD + HD + 127) // 128
            lo, hi = first * 128, last * 128
            col = lo + lax.broadcasted_iota(jnp.int32, (SPAN, hi - lo), 1)
            mine = (col >= h * HD) & (col < h * HD + HD)
            part = query[:, lo:hi]
            part = jnp.where(mine, part, jnp.zeros_like(part))
            scores = lax.dot_general(
                part, k_ref[s, :, lo:hi], (((1,), (1,)), ((), ())),
                preferred_element_type=jnp.float32,
            ) * scale
            scores = jnp.where(visible, scores, NEG)
            top = jnp.max(scores, axis=1, keepdims=True)
            weights = jnp.where(visible, jnp.exp(scores - top), 0.0)
            total = jnp.sum(weights, axis=1, keepdims=True)
            mixed = jnp.dot(
                weights.astype(jnp.bfloat16), v_ref[s, :, lo:hi],
                preferred_element_type=jnp.float32,
            )
            some = total > 0.0
            safe = jnp.where(some, total, 1.0)
            mixed = jnp.where(mine, mixed * (1.0 / safe), 0.0)
            for t in range(first, last):
                tiles[t] = tiles[t] + mixed[:, t * 128 - lo : t * 128 - lo + 128]
            level = jnp.where(some, top + jnp.log(safe), NEG)
            lse = jnp.where(lane // 4 == h, level, lse)
        if before is None:
            before = (used, request)

            @pl.when(used)
            def _():
                for t in range(FEATS // 128):
                    out_ref[request, :, t * 128 : t * 128 + 128] = tiles[t].astype(jnp.bfloat16)
                out_ref[request, :, FEATS:] = split_parts(lse)

            first_tiles, first_lse = tiles, lse
        else:
            same = before[0] & used & (before[1] == request)
            held = jnp.where(same, first_lse, NEG)
            best = jnp.maximum(held, lse)
            keep, take = jnp.exp(held - best), jnp.exp(lse - best)
            mass = keep + take
            keep, take = keep / mass, take / mass
            level = best + jnp.log(mass)

            @pl.when(used)
            def _():
                for t in range(FEATS // 128):
                    col = t * 128 + lane
                    k_b = jnp.zeros((SPAN, 128), jnp.float32)
                    t_b = jnp.zeros((SPAN, 128), jnp.float32)
                    for h in range(HEADS_DEV):
                        if h * HD < t * 128 + 128 and h * HD + HD > t * 128:
                            mine = (col >= h * HD) & (col < h * HD + HD)
                            k_b = jnp.where(mine, keep[:, 4 * h : 4 * h + 1], k_b)
                            t_b = jnp.where(mine, take[:, 4 * h : 4 * h + 1], t_b)
                    merged = first_tiles[t] * k_b + tiles[t] * t_b
                    out_ref[request, :, t * 128 : t * 128 + 128] = merged.astype(jnp.bfloat16)
                out_ref[request, :, FEATS:] = split_parts(level)


def spread(columns, width):
    row = lax.broadcasted_iota(jnp.int32, (128, columns), 0)
    col = lax.broadcasted_iota(jnp.int32, (128, columns), 1)
    hit = (row // 4 == col // width) & (row < 4 * HEADS_DEV)
    return jnp.where(hit, 1.0, 0.0).astype(jnp.bfloat16)


def finish_kernel(
    part_ref, w_ref, gain_ref, out_ref,
    recv_a, comb, recv_b, w_all, attn_own, attn_all, proj, recv_p, ssq_own, recv_s,
    sa_send, sa_recv, sb_send, sb_recv, sw_send, sw_recv, sg_send, sg_recv,
    sp_send, sp_recv, ss_send, ss_recv, diag_sem,
):
    me = lax.axis_index("ctx")
    tensor = lax.axis_index("tensor")
    x, j = me // PLANE, me % PLANE
    group, y = me // YS, me % YS
    barrier = pltpu.get_barrier_semaphore()
    off_diag = group != tensor

    def greet_plane(k, c):
        signal(barrier, {"ctx": x * PLANE + (j + k) % PLANE})
        return c

    def greet_eight(k, c):
        signal(barrier, {"ctx": (group + k) % GROUPS * YS + y})
        signal(barrier, {"tensor": (tensor + k) % GROUPS})
        signal(barrier, {"tensor": (group + GROUPS - k) % GROUPS, "ctx": tensor * YS + y})
        return c

    lax.fori_loop(1, PLANE, greet_plane, 0)
    lax.fori_loop(1, GROUPS, greet_eight, 0)

    @pl.when(off_diag)
    def _():
        signal(barrier, {"tensor": group, "ctx": tensor * YS + y})

    pl.semaphore_wait(barrier, PLANE - 1 + 3 * (GROUPS - 1) + off_diag.astype(jnp.int32))

    def to_x(dx):
        there = (x + dx) % REQS
        return remote(
            part_ref.at[there], recv_a.at[dx - 1], sa_send.at[dx - 1], sa_recv.at[dx - 1],
            {"ctx": there * PLANE + j},
        )

    for dx in range(1, REQS):
        to_x(dx).start()

    def to_y(k):
        return remote(
            w_ref, w_all.at[y], sw_send.at[k], sw_recv.at[k], {"ctx": group * YS + (y + k) % YS}
        )

    def start_y(k, c):
        to_y(k).start()
        return c

    lax.fori_loop(1, YS, start_y, 0)
    own_w = pltpu.make_async_copy(w_ref, w_all.at[y], diag_sem)
    own_w.start()

    to_heads = spread(FEATS, HD)
    to_lanes = spread(128, 4)

    def level_of(parts, pick):
        return jnp.dot(parts, pick, preferred_element_type=jnp.float32)

    for dx in range(1, REQS):
        to_x(dx).wait_recv()

    def to_plane(k):
        there = x * PLANE + (j + k) % PLANE
        return remote(comb.at[k], recv_b.at[k], sb_send.at[k], sb_recv.at[k], {"ctx": there})

    def combine(k):
        rows = pl.ds(pl.multiple_of((j + k) % PLANE * ROWS, ROWS), ROWS)
        blocks = [part_ref[x, rows, :]] + [recv_a[i, rows, :] for i in range(REQS - 1)]
        parts = [b[:, FEATS:] for b in blocks]
        wide = [level_of(p, to_heads) for p in parts]
        best = functools.reduce(jnp.maximum, wide)
        factors = [jnp.exp(w - best) for w in wide]
        mass = sum(factors)
        mixed = sum(b[:, :FEATS].astype(jnp.float32) * f for b, f in zip(blocks, factors))
        narrow = [level_of(p, to_lanes) for p in parts]
        top = functools.reduce(jnp.maximum, narrow)
        level = top + jnp.log(sum(jnp.exp(n - top) for n in narrow))
        return (mixed / mass).astype(jnp.bfloat16), split_parts(level)

    def reduce_x(k, c):
        mixed, parts = combine(k)
        comb[k, :, :FEATS] = mixed
        comb[k, :, FEATS:] = parts
        to_plane(k).start()
        return c

    lax.fori_loop(1, PLANE, reduce_x, 0)
    own_mixed, own_parts = combine(0)
    recv_b[0, :, :FEATS] = own_mixed
    recv_b[0, :, FEATS:] = own_parts

    def arrive_b(k, c):
        to_plane(k).wait_recv()
        return c

    lax.fori_loop(1, PLANE, arrive_b, 0)
    levels = level_of(recv_b[:, :, FEATS:].reshape(PLANE * ROWS, 128), to_heads)
    levels = levels.reshape(PLANE, ROWS, FEATS)
    best = jnp.max(levels, axis=0)
    factors = jnp.exp(levels - best[None])
    mass = jnp.sum(factors, axis=0)
    mixed = jnp.sum(recv_b[:, :, :FEATS].astype(jnp.float32) * factors, axis=0)
    attn = (mixed / mass).astype(jnp.bfloat16)
    attn_own[...] = attn

    def to_group(k):
        return remote(
            attn_own, attn_all.at[group], sg_send.at[k], sg_recv.at[k],
            {"ctx": (group + k) % GROUPS * YS + y},
        )

    def start_group(k, c):
        to_group(k).start()
        return c

    lax.fori_loop(1, GROUPS, start_group, 0)
    attn_all[group] = attn
    own_w.wait()

    def arrive_g(k, c):
        to_y(k).wait_recv()
        to_group(k).wait_recv()
        return c

    lax.fori_loop(1, GROUPS, arrive_g, 0)
    partial = lax.dot_general(
        attn_all[...].reshape(GROUPS * ROWS, FEATS), w_all[...].reshape(FEATS, FEATS),
        (((1,), (1,)), ((), ())), preferred_element_type=jnp.float32,
    )
    proj[...] = partial.astype(jnp.bfloat16).reshape(GROUPS, ROWS, FEATS)

    def to_owner(k):
        there = (tensor + k) % GROUPS
        return remote(
            proj.at[there], recv_p.at[k], sp_send.at[k], sp_recv.at[k],
            {"tensor": group, "ctx": there * YS + y},
        )

    def start_owner(k, c):
        to_owner(k).start()
        return c

    lax.fori_loop(1, GROUPS, start_owner, 0)

    @pl.when(off_diag)
    def _():
        to_owner(0).start()
        to_owner(0).wait_recv()

    @pl.when(jnp.logical_not(off_diag))
    def _():
        recv_p[0] = proj[tensor]

    def arrive_p(k, c):
        to_owner(k).wait_recv()
        return c

    lax.fori_loop(1, GROUPS, arrive_p, 0)
    summed = jnp.sum(recv_p[...].astype(jnp.float32), axis=0)
    squares = jnp.broadcast_to(jnp.sum(summed * summed, axis=1, keepdims=True), (ROWS, 128))
    ssq_own[...] = squares

    def to_tensor(k):
        return remote(
            ssq_own, recv_s.at[k], ss_send.at[k], ss_recv.at[k],
            {"tensor": (tensor + k) % GROUPS},
        )

    def start_tensor(k, c):
        to_tensor(k).start()
        return c

    lax.fori_loop(1, GROUPS, start_tensor, 0)
    recv_s[0] = squares

    def arrive_s(k, c):
        to_tensor(k).wait_recv()
        return c

    lax.fori_loop(1, GROUPS, arrive_s, 0)
    total = jnp.sum(recv_s[...], axis=0)[:, :1]
    inverse = lax.rsqrt(total * (1.0 / D) + 1e-05)
    out_ref[...] = (summed * inverse * gain_ref[...]).astype(jnp.bfloat16)

    for dx in range(1, REQS):
        to_x(dx).wait_send()

    def sent_plane(k, c):
        to_plane(k).wait_send()
        return c

    def sent_eight(k, c):
        to_y(k).wait_send()
        to_group(k).wait_send()
        to_owner(k).wait_send()
        to_tensor(k).wait_send()
        return c

    lax.fori_loop(1, PLANE, sent_plane, 0)
    lax.fori_loop(1, GROUPS, sent_eight, 0)

    @pl.when(off_diag)
    def _():
        to_owner(0).wait_send()


def body(queries, key_cache, value_cache, cached_len, block_slot, out_weight, norm_gain):
    vmem = pl.BlockSpec(memory_space=pltpu.VMEM)
    smem = pl.BlockSpec(memory_space=pltpu.SMEM)
    dma = pltpu.SemaphoreType.DMA
    bf16, f32 = jnp.bfloat16, jnp.float32
    n_ctx = REQS * PLANE
    weight_rows = out_weight.T
    gathered = pl.pallas_call(
        gather_kernel,
        out_shape=jax.ShapeDtypeStruct((n_ctx, ROWS, FEATS), bf16),
        in_specs=[vmem],
        out_specs=vmem,
        scratch_shapes=[dma, dma((PLANE,)), dma((REQS - 1, PLANE)), dma((n_ctx,))],
        compiler_params=pltpu.CompilerParams(collective_id=0, has_side_effects=True),
        name="gather_queries",
    )(queries)
    parts = pl.pallas_call(
        attention_kernel,
        out_shape=jax.ShapeDtypeStruct((REQS, SPAN, WIDE), bf16),
        in_specs=[smem, smem, vmem, vmem, vmem],
        out_specs=vmem,
        name="attention",
    )(block_slot, cached_len, gathered.reshape(n_ctx * ROWS, FEATS), key_cache, value_cache)
    return pl.pallas_call(
        finish_kernel,
        out_shape=jax.ShapeDtypeStruct((ROWS, FEATS), bf16),
        in_specs=[vmem] * 3,
        out_specs=vmem,
        scratch_shapes=[
            pltpu.VMEM((REQS - 1, SPAN, WIDE), bf16),
            pltpu.VMEM((PLANE, ROWS, WIDE), bf16),
            pltpu.VMEM((PLANE, ROWS, WIDE), bf16),
            pltpu.VMEM((YS, FEATS // YS, FEATS), bf16),
            pltpu.VMEM((ROWS, FEATS), bf16),
            pltpu.VMEM((GROUPS, ROWS, FEATS), bf16),
            pltpu.VMEM((GROUPS, ROWS, FEATS), bf16),
            pltpu.VMEM((GROUPS, ROWS, FEATS), bf16),
            pltpu.VMEM((ROWS, 128), f32),
            pltpu.VMEM((GROUPS, ROWS, 128), f32),
            dma((REQS - 1,)), dma((REQS - 1,)),
            dma((PLANE,)), dma((PLANE,)),
            dma((YS,)), dma((YS,)),
            dma((GROUPS,)), dma((GROUPS,)),
            dma((GROUPS,)), dma((GROUPS,)),
            dma((GROUPS,)), dma((GROUPS,)),
            dma,
        ],
        compiler_params=pltpu.CompilerParams(collective_id=1, has_side_effects=True),
        name="merge_project_norm",
    )(parts, weight_rows, norm_gain.reshape(1, FEATS))


def solution(mesh):
    in_specs = (
        P("ctx", "tensor"),
        P("ctx", None, "tensor"),
        P("ctx", None, "tensor"),
        P(),
        P(),
        P("tensor", "ctx"),
        P("tensor"),
    )
    out_specs = P("ctx", "tensor")
    return jax.shard_map(body, mesh=mesh, in_specs=in_specs, out_specs=out_specs, check_vma=False)
```

```python
import functools
import math

import jax
import jax.numpy as jnp
from jax import lax
from jax.experimental import pallas as pl
from jax.experimental.pallas import tpu as pltpu
from jax.sharding import PartitionSpec as P

HD = 96
REQS = 4
HEADS_DEV = 4
FEATS = 384
SPAN = 256
PLANE = 16
ROWS = 16
YS = 8
GROUPS = 8
D = 3072
NEG = -1e30
WIDE = FEATS + 128


def remote(src, dst, send, recv, device):
    return pltpu.make_async_remote_copy(
        src_ref=src,
        dst_ref=dst,
        send_sem=send,
        recv_sem=recv,
        device_id=device,
        device_id_type=pl.DeviceIdType.MESH,
    )


def signal(sem, device):
    pl.semaphore_signal(sem, inc=1, device_id=device, device_id_type=pl.DeviceIdType.MESH)


def gather_kernel(q_ref, out_ref, own_sem, send_plane, send_near, send_far, recv):
    me = lax.axis_index("ctx")
    x, j = me // PLANE, me % PLANE
    up, down = (x + 1) % REQS, (x + REQS - 1) % REQS
    barrier = pltpu.get_barrier_semaphore()

    def greet(k, c):
        signal(barrier, {"ctx": x * PLANE + (j + k) % PLANE})
        return c

    lax.fori_loop(1, PLANE, greet, 0)
    for there in (up, down):
        signal(barrier, {"ctx": there * PLANE + j})
    own = pltpu.make_async_copy(q_ref, out_ref.at[me], own_sem)
    own.start()
    pl.semaphore_wait(barrier, PLANE - 1 + 2)

    def block_of(plane, k):
        return plane * PLANE + (j + PLANE - k) % PLANE

    def to_plane(k):
        there = x * PLANE + (j + k) % PLANE
        return remote(q_ref, out_ref.at[me], send_plane.at[k], recv.at[me], {"ctx": there})

    def pass_on(plane, there, k, sem):
        block = block_of(plane, k)
        src = q_ref if isinstance(k, int) and k == 0 and plane is x else out_ref.at[block]
        return remote(src, out_ref.at[block], sem, recv.at[block], {"ctx": there * PLANE + j})

    def near(k):
        return [pass_on(x, up, k, send_near.at[0, k]), pass_on(x, down, k, send_near.at[1, k])]

    def far(i):
        return [
            pass_on(down, up, 2 * i, send_far.at[2 * i]),
            pass_on(up, down, 2 * i + 1, send_far.at[2 * i + 1]),
        ]

    def arrived(plane, k):
        block = block_of(plane, k)
        pltpu.make_async_copy(out_ref.at[block], out_ref.at[block], recv.at[block]).wait()

    def start_plane(k, c):
        to_plane(k).start()
        return c

    for copy in near(0):
        copy.start()
    lax.fori_loop(1, PLANE, start_plane, 0)

    def forward(k):
        arrived(x, k)
        for copy in near(k):
            copy.start()

    def relay(i):
        arrived(down, 2 * i)
        far(i)[0].start()
        arrived(up, 2 * i + 1)
        far(i)[1].start()

    forward(1)

    def step(i, c):
        forward(2 * i)
        forward(2 * i + 1)
        relay(i - 1)
        return c

    lax.fori_loop(1, PLANE // 2, step, 0)
    relay(PLANE // 2 - 1)

    def rest(i, c):
        arrived(down, 2 * i + 1)
        arrived(up, 2 * i)
        arrived((x + 2) % REQS, 2 * i)
        arrived((x + 2) % REQS, 2 * i + 1)
        for copy in far(i):
            copy.wait_send()
        return c

    lax.fori_loop(0, PLANE // 2, rest, 0)

    def sent(k, c):
        to_plane(k).wait_send()
        for copy in near(k):
            copy.wait_send()
        return c

    lax.fori_loop(1, PLANE, sent, 0)
    for copy in near(0):
        copy.wait_send()
    own.wait()


def split_parts(lse):
    lane = lax.broadcasted_iota(jnp.int32, lse.shape, 1)
    high = lse.astype(jnp.bfloat16).astype(jnp.float32)
    rest = lse - high
    mid = rest.astype(jnp.bfloat16).astype(jnp.float32)
    low = rest - mid
    part = lane % 4
    picked = jnp.where(part == 0, high, jnp.where(part == 1, mid, jnp.where(part == 2, low, 0.0)))
    return jnp.where(lane < 4 * HEADS_DEV, picked, 0.0).astype(jnp.bfloat16)


def attention_kernel(table_ref, len_ref, q_ref, k_ref, v_ref, out_ref):
    slots = k_ref.shape[0]
    block_rows = k_ref.shape[1]
    me = lax.axis_index("ctx")
    scale = 1.0 / math.sqrt(HD)
    empty_parts = split_parts(jnp.full((SPAN, 128), NEG, jnp.float32))
    for r in range(REQS):
        out_ref[r, :, :FEATS] = jnp.zeros((SPAN, FEATS), jnp.bfloat16)
        out_ref[r, :, FEATS:] = empty_parts
    before = None
    for s in range(slots):
        slot_id = me * slots + s
        found = jnp.int32(-1)
        for r in range(REQS):
            for b in range(table_ref.shape[1]):
                found = jnp.where(table_ref[r, b] == slot_id, r * 16 + b, found)
        used = found >= 0
        request = jnp.where(used, found // 16, 0)
        first_key = jnp.where(used, found % 16 * block_rows, 1 << 28)
        diff = (
            lax.broadcasted_iota(jnp.int32, (SPAN, block_rows), 1)
            - lax.broadcasted_iota(jnp.int32, (SPAN, block_rows), 0)
        )
        visible = diff <= len_ref[request] - first_key
        query = q_ref[pl.ds(pl.multiple_of(request * SPAN, SPAN), SPAN), :]
        tiles = [jnp.zeros((SPAN, 128), jnp.float32) for _ in range(FEATS // 128)]
        lane = lax.broadcasted_iota(jnp.int32, (SPAN, 128), 1)
        lse = jnp.full((SPAN, 128), NEG, jnp.float32)
        for h in range(HEADS_DEV):
            first, last = h * HD // 128, (h * HD + HD + 127) // 128
            lo, hi = first * 128, last * 128
            col = lo + lax.broadcasted_iota(jnp.int32, (SPAN, hi - lo), 1)
            mine = (col >= h * HD) & (col < h * HD + HD)
            part = query[:, lo:hi]
            part = jnp.where(mine, part, jnp.zeros_like(part))
            scores = lax.dot_general(
                part, k_ref[s, :, lo:hi], (((1,), (1,)), ((), ())),
                preferred_element_type=jnp.float32,
            ) * scale
            scores = jnp.where(visible, scores, NEG)
            top = jnp.max(scores, axis=1, keepdims=True)
            weights = jnp.where(visible, jnp.exp(scores - top), 0.0)
            total = jnp.sum(weights, axis=1, keepdims=True)
            mixed = jnp.dot(
                weights.astype(jnp.bfloat16), v_ref[s, :, lo:hi],
                preferred_element_type=jnp.float32,
            )
            some = total > 0.0
            safe = jnp.where(some, total, 1.0)
            mixed = jnp.where(mine, mixed * (1.0 / safe), 0.0)
            for t in range(first, last):
                tiles[t] = tiles[t] + mixed[:, t * 128 - lo : t * 128 - lo + 128]
            level = jnp.where(some, top + jnp.log(safe), NEG)
            lse = jnp.where(lane // 4 == h, level, lse)
        if before is None:
            before = (used, request)

            @pl.when(used)
            def _():
                for t in range(FEATS // 128):
                    out_ref[request, :, t * 128 : t * 128 + 128] = tiles[t].astype(jnp.bfloat16)
                out_ref[request, :, FEATS:] = split_parts(lse)

            first_tiles, first_lse = tiles, lse
        else:
            same = before[0] & used & (before[1] == request)
            held = jnp.where(same, first_lse, NEG)
            best = jnp.maximum(held, lse)
            keep, take = jnp.exp(held - best), jnp.exp(lse - best)
            mass = keep + take
            keep, take = keep / mass, take / mass
            level = best + jnp.log(mass)

            @pl.when(used)
            def _():
                for t in range(FEATS // 128):
                    col = t * 128 + lane
                    k_b = jnp.zeros((SPAN, 128), jnp.float32)
                    t_b = jnp.zeros((SPAN, 128), jnp.float32)
                    for h in range(HEADS_DEV):
                        if h * HD < t * 128 + 128 and h * HD + HD > t * 128:
                            mine = (col >= h * HD) & (col < h * HD + HD)
                            k_b = jnp.where(mine, keep[:, 4 * h : 4 * h + 1], k_b)
                            t_b = jnp.where(mine, take[:, 4 * h : 4 * h + 1], t_b)
                    merged = first_tiles[t] * k_b + tiles[t] * t_b
                    out_ref[request, :, t * 128 : t * 128 + 128] = merged.astype(jnp.bfloat16)
                out_ref[request, :, FEATS:] = split_parts(level)


def spread(columns, width):
    row = lax.broadcasted_iota(jnp.int32, (128, columns), 0)
    col = lax.broadcasted_iota(jnp.int32, (128, columns), 1)
    hit = (row // 4 == col // width) & (row < 4 * HEADS_DEV)
    return jnp.where(hit, 1.0, 0.0).astype(jnp.bfloat16)


def finish_kernel(
    part_ref, w_ref, gain_ref, out_ref,
    relay_in, relay_out, recv_a, comb, recv_b, w_all, attn_own, attn_all, proj, recv_p, ssq_own, recv_s,
    sr_send, sr_recv, sa_send, sa_recv, sb_send, sb_recv, sw_send, sw_recv, sg_send, sg_recv,
    sp_send, sp_recv, ss_send, ss_recv, diag_sem,
):
    me = lax.axis_index("ctx")
    tensor = lax.axis_index("tensor")
    x, j = me // PLANE, me % PLANE
    group, y = me // YS, me % YS
    barrier = pltpu.get_barrier_semaphore()
    off_diag = group != tensor

    def greet_plane(k, c):
        signal(barrier, {"ctx": x * PLANE + (j + k) % PLANE})
        return c

    def greet_eight(k, c):
        signal(barrier, {"ctx": (group + k) % GROUPS * YS + y})
        signal(barrier, {"tensor": (tensor + k) % GROUPS})
        signal(barrier, {"tensor": (group + GROUPS - k) % GROUPS, "ctx": tensor * YS + y})
        return c

    lax.fori_loop(1, PLANE, greet_plane, 0)
    lax.fori_loop(1, GROUPS, greet_eight, 0)

    @pl.when(off_diag)
    def _():
        signal(barrier, {"tensor": group, "ctx": tensor * YS + y})

    pl.semaphore_wait(barrier, PLANE - 1 + 3 * (GROUPS - 1) + off_diag.astype(jnp.int32))

    half = PLANE // 2
    toward = ((x + 1) % REQS, (x + REQS - 1) % REQS)

    def rows_of(k):
        return pl.ds(pl.multiple_of((j + k) % PLANE * ROWS, ROWS), ROWS)

    def to_relay(way, i):
        return remote(
            part_ref.at[(x + 2) % REQS, rows_of(2 * i + way)], relay_in.at[way, i],
            sr_send.at[way, i], sr_recv.at[way, i], {"ctx": toward[way] * PLANE + j},
        )

    def to_near(way, i, relayed):
        k = 2 * i + (way if relayed else 1 - way)
        src = relay_out.at[way, i] if relayed else part_ref.at[toward[way], rows_of(k)]
        return remote(
            src, recv_a.at[way, k], sa_send.at[way, k], sa_recv.at[way, k],
            {"ctx": toward[way] * PLANE + j},
        )

    def start_relays(t, c):
        for way in range(2):
            to_relay(way, (t + 1) % half).start()
        return c

    def start_near(t, c):
        for way in range(2):
            to_near(way, (t + 1) % half, False).start()
        return c

    lax.fori_loop(0, half, start_relays, 0)
    lax.fori_loop(0, half, start_near, 0)

    def to_y(k):
        return remote(
            w_ref, w_all.at[y], sw_send.at[k], sw_recv.at[k], {"ctx": group * YS + (y + k) % YS}
        )

    def start_y(k, c):
        to_y(k).start()
        return c

    lax.fori_loop(1, YS, start_y, 0)
    own_w = pltpu.make_async_copy(w_ref, w_all.at[y], diag_sem)
    own_w.start()

    to_heads = spread(FEATS, HD)
    to_lanes = spread(128, 4)

    def level_of(parts, pick):
        return jnp.dot(parts, pick, preferred_element_type=jnp.float32)

    def to_plane(k):
        there = x * PLANE + (j + k) % PLANE
        return remote(comb.at[k], recv_b.at[k], sb_send.at[k], sb_recv.at[k], {"ctx": there})

    def combine(blocks):
        parts = [b[:, FEATS:] for b in blocks]
        wide = [level_of(p, to_heads) for p in parts]
        best = functools.reduce(jnp.maximum, wide)
        factors = [jnp.exp(w - best) for w in wide]
        mass = sum(factors)
        mixed = sum(b[:, :FEATS].astype(jnp.float32) * f for b, f in zip(blocks, factors))
        narrow = [level_of(p, to_lanes) for p in parts]
        top = functools.reduce(jnp.maximum, narrow)
        level = top + jnp.log(sum(jnp.exp(n - top) for n in narrow))
        return (mixed / mass).astype(jnp.bfloat16), split_parts(level)

    def relay(t, c):
        i = (t + 1) % half
        for way in range(2):
            to_relay(way, i).wait_recv()
        merged = [
            combine([relay_in[way, i], part_ref[toward[way], rows_of(2 * i + way), :]])
            for way in range(2)
        ]
        for way in range(2):
            relay_out[way, i, :, :FEATS] = merged[way][0]
            relay_out[way, i, :, FEATS:] = merged[way][1]
        for way in range(2):
            to_near(way, i, True).start()
        return c

    lax.fori_loop(0, half, relay, 0)

    def owned(i):
        for way in range(2):
            to_near(way, i, False).wait_recv()
            to_near(way, i, True).wait_recv()
        return [
            combine([part_ref[x, rows_of(k), :], recv_a[0, k], recv_a[1, k]])
            for k in (2 * i, 2 * i + 1)
        ]

    def reduce_x(i, c):
        merged = owned(i)
        for at in range(2):
            comb[2 * i + at, :, :FEATS] = merged[at][0]
            comb[2 * i + at, :, FEATS:] = merged[at][1]
        for at in range(2):
            to_plane(2 * i + at).start()
        return c

    lax.fori_loop(1, half, reduce_x, 0)
    merged = owned(0)
    comb[1, :, :FEATS] = merged[1][0]
    comb[1, :, FEATS:] = merged[1][1]
    to_plane(1).start()
    recv_b[0, :, :FEATS] = merged[0][0]
    recv_b[0, :, FEATS:] = merged[0][1]

    def arrive_b(k, c):
        to_plane(k).wait_recv()
        return c

    lax.fori_loop(1, PLANE, arrive_b, 0)
    levels = level_of(recv_b[:, :, FEATS:].reshape(PLANE * ROWS, 128), to_heads)
    levels = levels.reshape(PLANE, ROWS, FEATS)
    best = jnp.max(levels, axis=0)
    factors = jnp.exp(levels - best[None])
    mass = jnp.sum(factors, axis=0)
    mixed = jnp.sum(recv_b[:, :, :FEATS].astype(jnp.float32) * factors, axis=0)
    attn = (mixed / mass).astype(jnp.bfloat16)
    attn_own[...] = attn

    def to_group(k):
        return remote(
            attn_own, attn_all.at[group], sg_send.at[k], sg_recv.at[k],
            {"ctx": (group + k) % GROUPS * YS + y},
        )

    def start_group(k, c):
        to_group(k).start()
        return c

    lax.fori_loop(1, GROUPS, start_group, 0)
    attn_all[group] = attn
    own_w.wait()

    def arrive_g(k, c):
        to_y(k).wait_recv()
        to_group(k).wait_recv()
        return c

    lax.fori_loop(1, GROUPS, arrive_g, 0)
    partial = lax.dot_general(
        attn_all[...].reshape(GROUPS * ROWS, FEATS), w_all[...].reshape(FEATS, FEATS),
        (((1,), (1,)), ((), ())), preferred_element_type=jnp.float32,
    )
    proj[...] = partial.astype(jnp.bfloat16).reshape(GROUPS, ROWS, FEATS)

    def to_owner(k):
        there = (tensor + k) % GROUPS
        return remote(
            proj.at[there], recv_p.at[k], sp_send.at[k], sp_recv.at[k],
            {"tensor": group, "ctx": there * YS + y},
        )

    def start_owner(k, c):
        to_owner(k).start()
        return c

    lax.fori_loop(1, GROUPS, start_owner, 0)

    @pl.when(off_diag)
    def _():
        to_owner(0).start()
        to_owner(0).wait_recv()

    @pl.when(jnp.logical_not(off_diag))
    def _():
        recv_p[0] = proj[tensor]

    def arrive_p(k, c):
        to_owner(k).wait_recv()
        return c

    lax.fori_loop(1, GROUPS, arrive_p, 0)
    summed = jnp.sum(recv_p[...].astype(jnp.float32), axis=0)
    squares = jnp.broadcast_to(jnp.sum(summed * summed, axis=1, keepdims=True), (ROWS, 128))
    ssq_own[...] = squares

    def to_tensor(k):
        return remote(
            ssq_own, recv_s.at[k], ss_send.at[k], ss_recv.at[k],
            {"tensor": (tensor + k) % GROUPS},
        )

    def start_tensor(k, c):
        to_tensor(k).start()
        return c

    lax.fori_loop(1, GROUPS, start_tensor, 0)
    recv_s[0] = squares

    def arrive_s(k, c):
        to_tensor(k).wait_recv()
        return c

    lax.fori_loop(1, GROUPS, arrive_s, 0)
    total = jnp.sum(recv_s[...], axis=0)[:, :1]
    inverse = lax.rsqrt(total * (1.0 / D) + 1e-05)
    out_ref[...] = (summed * inverse * gain_ref[...]).astype(jnp.bfloat16)

    def sent_a(i, c):
        for way in range(2):
            to_relay(way, i).wait_send()
            to_near(way, i, False).wait_send()
            to_near(way, i, True).wait_send()
        return c

    lax.fori_loop(0, half, sent_a, 0)

    def sent_plane(k, c):
        to_plane(k).wait_send()
        return c

    def sent_eight(k, c):
        to_y(k).wait_send()
        to_group(k).wait_send()
        to_owner(k).wait_send()
        to_tensor(k).wait_send()
        return c

    lax.fori_loop(1, PLANE, sent_plane, 0)
    lax.fori_loop(1, GROUPS, sent_eight, 0)

    @pl.when(off_diag)
    def _():
        to_owner(0).wait_send()


def body(queries, key_cache, value_cache, cached_len, block_slot, out_weight, norm_gain):
    vmem = pl.BlockSpec(memory_space=pltpu.VMEM)
    smem = pl.BlockSpec(memory_space=pltpu.SMEM)
    dma = pltpu.SemaphoreType.DMA
    bf16, f32 = jnp.bfloat16, jnp.float32
    n_ctx = REQS * PLANE
    weight_rows = out_weight.T
    gathered = pl.pallas_call(
        gather_kernel,
        out_shape=jax.ShapeDtypeStruct((n_ctx, ROWS, FEATS), bf16),
        in_specs=[vmem],
        out_specs=vmem,
        scratch_shapes=[dma, dma((PLANE,)), dma((2, PLANE)), dma((PLANE,)), dma((n_ctx,))],
        compiler_params=pltpu.CompilerParams(collective_id=0, has_side_effects=True),
        name="gather_queries",
    )(queries)
    parts = pl.pallas_call(
        attention_kernel,
        out_shape=jax.ShapeDtypeStruct((REQS, SPAN, WIDE), bf16),
        in_specs=[smem, smem, vmem, vmem, vmem],
        out_specs=vmem,
        name="attention",
    )(block_slot, cached_len, gathered.reshape(n_ctx * ROWS, FEATS), key_cache, value_cache)
    return pl.pallas_call(
        finish_kernel,
        out_shape=jax.ShapeDtypeStruct((ROWS, FEATS), bf16),
        in_specs=[vmem] * 3,
        out_specs=vmem,
        scratch_shapes=[
            pltpu.VMEM((2, PLANE // 2, ROWS, WIDE), bf16),
            pltpu.VMEM((2, PLANE // 2, ROWS, WIDE), bf16),
            pltpu.VMEM((2, PLANE, ROWS, WIDE), bf16),
            pltpu.VMEM((PLANE, ROWS, WIDE), bf16),
            pltpu.VMEM((PLANE, ROWS, WIDE), bf16),
            pltpu.VMEM((YS, FEATS // YS, FEATS), bf16),
            pltpu.VMEM((ROWS, FEATS), bf16),
            pltpu.VMEM((GROUPS, ROWS, FEATS), bf16),
            pltpu.VMEM((GROUPS, ROWS, FEATS), bf16),
            pltpu.VMEM((GROUPS, ROWS, FEATS), bf16),
            pltpu.VMEM((ROWS, 128), f32),
            pltpu.VMEM((GROUPS, ROWS, 128), f32),
            dma((2, PLANE // 2)), dma((2, PLANE // 2)),
            dma((2, PLANE)), dma((2, PLANE)),
            dma((PLANE,)), dma((PLANE,)),
            dma((YS,)), dma((YS,)),
            dma((GROUPS,)), dma((GROUPS,)),
            dma((GROUPS,)), dma((GROUPS,)),
            dma((GROUPS,)), dma((GROUPS,)),
            dma,
        ],
        compiler_params=pltpu.CompilerParams(collective_id=1, has_side_effects=True),
        name="merge_project_norm",
    )(parts, weight_rows, norm_gain.reshape(1, FEATS))


def solution(mesh):
    in_specs = (
        P("ctx", "tensor"),
        P("ctx", None, "tensor"),
        P("ctx", None, "tensor"),
        P(),
        P(),
        P("tensor", "ctx"),
        P("tensor"),
    )
    out_specs = P("ctx", "tensor")
    return jax.shard_map(body, mesh=mesh, in_specs=in_specs, out_specs=out_specs, check_vma=False)
```

```python
import functools
import math

import jax
import jax.numpy as jnp
from jax import lax
from jax.experimental import pallas as pl
from jax.experimental.pallas import tpu as pltpu
from jax.sharding import PartitionSpec as P

HD = 96
REQS = 4
HEADS_DEV = 4
FEATS = 384
SPAN = 256
PLANE = 16
ROWS = 16
YS = 8
GROUPS = 8
D = 3072
NEG = -1e30
WIDE = FEATS + 128


def remote(src, dst, send, recv, device):
    return pltpu.make_async_remote_copy(
        src_ref=src,
        dst_ref=dst,
        send_sem=send,
        recv_sem=recv,
        device_id=device,
        device_id_type=pl.DeviceIdType.MESH,
    )


def signal(sem, device):
    pl.semaphore_signal(sem, inc=1, device_id=device, device_id_type=pl.DeviceIdType.MESH)


def gather_kernel(q_ref, out_ref, own_sem, send_plane, send_x, recv):
    me = lax.axis_index("ctx")
    x, j = me // PLANE, me % PLANE
    barrier = pltpu.get_barrier_semaphore()

    def greet(k, c):
        signal(barrier, {"ctx": x * PLANE + (j + k) % PLANE})
        return c

    lax.fori_loop(1, PLANE, greet, 0)
    for dx in range(1, REQS):
        signal(barrier, {"ctx": (x + dx) % REQS * PLANE + j})
    own = pltpu.make_async_copy(q_ref, out_ref.at[me], own_sem)
    own.start()
    pl.semaphore_wait(barrier, PLANE - 1 + REQS - 1)

    def to_plane(k):
        there = x * PLANE + (j + k) % PLANE
        return remote(q_ref, out_ref.at[me], send_plane.at[k], recv.at[me], {"ctx": there})

    def to_x(k, dx):
        block = x * PLANE + (j + PLANE - k) % PLANE
        there = (x + dx) % REQS * PLANE + j
        src = q_ref if isinstance(k, int) and k == 0 else out_ref.at[block]
        return remote(
            src, out_ref.at[block], send_x.at[dx - 1, k], recv.at[block], {"ctx": there}
        )

    def start_plane(k, c):
        to_plane(k).start()
        return c

    for dx in range(1, REQS):
        to_x(0, dx).start()
    lax.fori_loop(1, PLANE, start_plane, 0)

    def forward(k, c):
        block = x * PLANE + (j + PLANE - k) % PLANE
        pltpu.make_async_copy(out_ref.at[block], out_ref.at[block], recv.at[block]).wait()
        for dx in range(1, REQS):
            to_x(k, dx).start()
        return c

    lax.fori_loop(1, PLANE, forward, 0)

    def arrive(k, c):
        for dx in range(1, REQS):
            block = (x + dx) % REQS * PLANE + (j + PLANE - k) % PLANE
            pltpu.make_async_copy(out_ref.at[block], out_ref.at[block], recv.at[block]).wait()
        return c

    lax.fori_loop(0, PLANE, arrive, 0)

    def sent(k, c):
        to_plane(k).wait_send()
        for dx in range(1, REQS):
            to_x(k, dx).wait_send()
        return c

    lax.fori_loop(1, PLANE, sent, 0)
    for dx in range(1, REQS):
        to_x(0, dx).wait_send()
    own.wait()


def split_parts(lse):
    lane = lax.broadcasted_iota(jnp.int32, lse.shape, 1)
    high = lse.astype(jnp.bfloat16).astype(jnp.float32)
    rest = lse - high
    mid = rest.astype(jnp.bfloat16).astype(jnp.float32)
    low = rest - mid
    part = lane % 4
    picked = jnp.where(part == 0, high, jnp.where(part == 1, mid, jnp.where(part == 2, low, 0.0)))
    return jnp.where(lane < 4 * HEADS_DEV, picked, 0.0).astype(jnp.bfloat16)


def attention_kernel(table_ref, len_ref, q_ref, k_ref, v_ref, out_ref):
    slots = k_ref.shape[0]
    block_rows = k_ref.shape[1]
    me = lax.axis_index("ctx")
    scale = 1.0 / math.sqrt(HD)
    empty_parts = split_parts(jnp.full((SPAN, 128), NEG, jnp.float32))
    for r in range(REQS):
        out_ref[r, :, :FEATS] = jnp.zeros((SPAN, FEATS), jnp.bfloat16)
        out_ref[r, :, FEATS:] = empty_parts
    before = None
    for s in range(slots):
        slot_id = me * slots + s
        found = jnp.int32(-1)
        for r in range(REQS):
            for b in range(table_ref.shape[1]):
                found = jnp.where(table_ref[r, b] == slot_id, r * 16 + b, found)
        used = found >= 0
        request = jnp.where(used, found // 16, 0)
        first_key = jnp.where(used, found % 16 * block_rows, 1 << 28)
        diff = (
            lax.broadcasted_iota(jnp.int32, (SPAN, block_rows), 1)
            - lax.broadcasted_iota(jnp.int32, (SPAN, block_rows), 0)
        )
        visible = diff <= len_ref[request] - first_key
        query = q_ref[pl.ds(pl.multiple_of(request * SPAN, SPAN), SPAN), :]
        tiles = [jnp.zeros((SPAN, 128), jnp.float32) for _ in range(FEATS // 128)]
        lane = lax.broadcasted_iota(jnp.int32, (SPAN, 128), 1)
        lse = jnp.full((SPAN, 128), NEG, jnp.float32)
        for h in range(HEADS_DEV):
            first, last = h * HD // 128, (h * HD + HD + 127) // 128
            lo, hi = first * 128, last * 128
            col = lo + lax.broadcasted_iota(jnp.int32, (SPAN, hi - lo), 1)
            mine = (col >= h * HD) & (col < h * HD + HD)
            part = query[:, lo:hi]
            part = jnp.where(mine, part, jnp.zeros_like(part))
            scores = lax.dot_general(
                part, k_ref[s, :, lo:hi], (((1,), (1,)), ((), ())),
                preferred_element_type=jnp.float32,
            ) * scale
            scores = jnp.where(visible, scores, NEG)
            top = jnp.max(scores, axis=1, keepdims=True)
            weights = jnp.where(visible, jnp.exp(scores - top), 0.0)
            total = jnp.sum(weights, axis=1, keepdims=True)
            mixed = jnp.dot(
                weights.astype(jnp.bfloat16), v_ref[s, :, lo:hi],
                preferred_element_type=jnp.float32,
            )
            some = total > 0.0
            safe = jnp.where(some, total, 1.0)
            mixed = jnp.where(mine, mixed * (1.0 / safe), 0.0)
            for t in range(first, last):
                tiles[t] = tiles[t] + mixed[:, t * 128 - lo : t * 128 - lo + 128]
            level = jnp.where(some, top + jnp.log(safe), NEG)
            lse = jnp.where(lane // 4 == h, level, lse)
        if before is None:
            before = (used, request)

            @pl.when(used)
            def _():
                for t in range(FEATS // 128):
                    out_ref[request, :, t * 128 : t * 128 + 128] = tiles[t].astype(jnp.bfloat16)
                out_ref[request, :, FEATS:] = split_parts(lse)

            first_tiles, first_lse = tiles, lse
        else:
            same = before[0] & used & (before[1] == request)
            held = jnp.where(same, first_lse, NEG)
            best = jnp.maximum(held, lse)
            keep, take = jnp.exp(held - best), jnp.exp(lse - best)
            mass = keep + take
            keep, take = keep / mass, take / mass
            level = best + jnp.log(mass)

            @pl.when(used)
            def _():
                for t in range(FEATS // 128):
                    col = t * 128 + lane
                    k_b = jnp.zeros((SPAN, 128), jnp.float32)
                    t_b = jnp.zeros((SPAN, 128), jnp.float32)
                    for h in range(HEADS_DEV):
                        if h * HD < t * 128 + 128 and h * HD + HD > t * 128:
                            mine = (col >= h * HD) & (col < h * HD + HD)
                            k_b = jnp.where(mine, keep[:, 4 * h : 4 * h + 1], k_b)
                            t_b = jnp.where(mine, take[:, 4 * h : 4 * h + 1], t_b)
                    merged = first_tiles[t] * k_b + tiles[t] * t_b
                    out_ref[request, :, t * 128 : t * 128 + 128] = merged.astype(jnp.bfloat16)
                out_ref[request, :, FEATS:] = split_parts(level)


def spread(columns, width):
    row = lax.broadcasted_iota(jnp.int32, (128, columns), 0)
    col = lax.broadcasted_iota(jnp.int32, (128, columns), 1)
    hit = (row // 4 == col // width) & (row < 4 * HEADS_DEV)
    return jnp.where(hit, 1.0, 0.0).astype(jnp.bfloat16)


def finish_kernel(
    part_ref, w_ref, gain_ref, out_ref,
    relay_in, relay_out, recv_a, comb, recv_b, w_all, attn_own, attn_all, proj, recv_p, ssq_own, recv_s,
    sr_send, sr_recv, sa_send, sa_recv, sb_send, sb_recv, sw_send, sw_recv, sg_send, sg_recv,
    sp_send, sp_recv, ss_send, ss_recv, diag_sem,
):
    me = lax.axis_index("ctx")
    tensor = lax.axis_index("tensor")
    x, j = me // PLANE, me % PLANE
    group, y = me // YS, me % YS
    barrier = pltpu.get_barrier_semaphore()
    off_diag = group != tensor

    def greet_plane(k, c):
        signal(barrier, {"ctx": x * PLANE + (j + k) % PLANE})
        return c

    def greet_eight(k, c):
        signal(barrier, {"ctx": (group + k) % GROUPS * YS + y})
        signal(barrier, {"tensor": (tensor + k) % GROUPS})
        signal(barrier, {"tensor": (group + GROUPS - k) % GROUPS, "ctx": tensor * YS + y})
        return c

    lax.fori_loop(1, PLANE, greet_plane, 0)
    lax.fori_loop(1, GROUPS, greet_eight, 0)

    @pl.when(off_diag)
    def _():
        signal(barrier, {"tensor": group, "ctx": tensor * YS + y})

    pl.semaphore_wait(barrier, PLANE - 1 + 3 * (GROUPS - 1) + off_diag.astype(jnp.int32))

    half = PLANE // 2
    toward = ((x + 1) % REQS, (x + REQS - 1) % REQS)

    def rows_of(k):
        return pl.ds(pl.multiple_of((j + k) % PLANE * ROWS, ROWS), ROWS)

    def to_relay(way, i):
        return remote(
            part_ref.at[(x + 2) % REQS, rows_of(2 * i + way)], relay_in.at[way, i],
            sr_send.at[way, i], sr_recv.at[way, i], {"ctx": toward[way] * PLANE + j},
        )

    def to_near(way, i, relayed):
        k = 2 * i + (way if relayed else 1 - way)
        src = relay_out.at[way, i] if relayed else part_ref.at[toward[way], rows_of(k)]
        return remote(
            src, recv_a.at[way, k], sa_send.at[way, k], sa_recv.at[way, k],
            {"ctx": toward[way] * PLANE + j},
        )

    def start_relays(t, c):
        for way in range(2):
            to_relay(way, (t + 1) % half).start()
        return c

    def start_near(t, c):
        for way in range(2):
            to_near(way, (t + 1) % half, False).start()
        return c

    lax.fori_loop(0, half, start_relays, 0)
    lax.fori_loop(0, half, start_near, 0)

    def to_y(k):
        return remote(
            w_ref, w_all.at[y], sw_send.at[k], sw_recv.at[k], {"ctx": group * YS + (y + k) % YS}
        )

    def start_y(k, c):
        to_y(k).start()
        return c

    lax.fori_loop(1, YS, start_y, 0)
    own_w = pltpu.make_async_copy(w_ref, w_all.at[y], diag_sem)
    own_w.start()

    to_heads = spread(FEATS, HD)
    to_lanes = spread(128, 4)

    def level_of(parts, pick):
        return jnp.dot(parts, pick, preferred_element_type=jnp.float32)

    def to_plane(k):
        there = x * PLANE + (j + k) % PLANE
        return remote(comb.at[k], recv_b.at[k], sb_send.at[k], sb_recv.at[k], {"ctx": there})

    def combine(blocks):
        parts = [b[:, FEATS:] for b in blocks]
        wide = [level_of(p, to_heads) for p in parts]
        best = functools.reduce(jnp.maximum, wide)
        factors = [jnp.exp(w - best) for w in wide]
        mass = sum(factors)
        mixed = sum(b[:, :FEATS].astype(jnp.float32) * f for b, f in zip(blocks, factors))
        narrow = [level_of(p, to_lanes) for p in parts]
        top = functools.reduce(jnp.maximum, narrow)
        level = top + jnp.log(sum(jnp.exp(n - top) for n in narrow))
        return (mixed / mass).astype(jnp.bfloat16), split_parts(level)

    def relay(t, c):
        i = (t + 1) % half
        for way in range(2):
            to_relay(way, i).wait_recv()
        merged = [
            combine([relay_in[way, i], part_ref[toward[way], rows_of(2 * i + way), :]])
            for way in range(2)
        ]
        for way in range(2):
            relay_out[way, i, :, :FEATS] = merged[way][0]
            relay_out[way, i, :, FEATS:] = merged[way][1]
        for way in range(2):
            to_near(way, i, True).start()
        return c

    lax.fori_loop(0, half, relay, 0)

    def owned(i):
        for way in range(2):
            to_near(way, i, False).wait_recv()
            to_near(way, i, True).wait_recv()
        return [
            combine([part_ref[x, rows_of(k), :], recv_a[0, k], recv_a[1, k]])
            for k in (2 * i, 2 * i + 1)
        ]

    def reduce_x(i, c):
        merged = owned(i)
        for at in range(2):
            comb[2 * i + at, :, :FEATS] = merged[at][0]
            comb[2 * i + at, :, FEATS:] = merged[at][1]
        for at in range(2):
            to_plane(2 * i + at).start()
        return c

    lax.fori_loop(1, half, reduce_x, 0)
    merged = owned(0)
    comb[1, :, :FEATS] = merged[1][0]
    comb[1, :, FEATS:] = merged[1][1]
    to_plane(1).start()
    recv_b[0, :, :FEATS] = merged[0][0]
    recv_b[0, :, FEATS:] = merged[0][1]

    def arrive_b(k, c):
        to_plane(k).wait_recv()
        return c

    lax.fori_loop(1, PLANE, arrive_b, 0)
    levels = level_of(recv_b[:, :, FEATS:].reshape(PLANE * ROWS, 128), to_heads)
    levels = levels.reshape(PLANE, ROWS, FEATS)
    best = jnp.max(levels, axis=0)
    factors = jnp.exp(levels - best[None])
    mass = jnp.sum(factors, axis=0)
    mixed = jnp.sum(recv_b[:, :, :FEATS].astype(jnp.float32) * factors, axis=0)
    attn = (mixed / mass).astype(jnp.bfloat16)
    attn_own[...] = attn

    def to_group(k):
        return remote(
            attn_own, attn_all.at[group], sg_send.at[k], sg_recv.at[k],
            {"ctx": (group + k) % GROUPS * YS + y},
        )

    def start_group(k, c):
        to_group(k).start()
        return c

    lax.fori_loop(1, GROUPS, start_group, 0)
    attn_all[group] = attn
    own_w.wait()

    def arrive_g(k, c):
        to_y(k).wait_recv()
        to_group(k).wait_recv()
        return c

    lax.fori_loop(1, GROUPS, arrive_g, 0)
    partial = lax.dot_general(
        attn_all[...].reshape(GROUPS * ROWS, FEATS), w_all[...].reshape(FEATS, FEATS),
        (((1,), (1,)), ((), ())), preferred_element_type=jnp.float32,
    )
    proj[...] = partial.astype(jnp.bfloat16).reshape(GROUPS, ROWS, FEATS)

    def to_owner(k):
        there = (tensor + k) % GROUPS
        return remote(
            proj.at[there], recv_p.at[k], sp_send.at[k], sp_recv.at[k],
            {"tensor": group, "ctx": there * YS + y},
        )

    def start_owner(k, c):
        to_owner(k).start()
        return c

    lax.fori_loop(1, GROUPS, start_owner, 0)

    @pl.when(off_diag)
    def _():
        to_owner(0).start()
        to_owner(0).wait_recv()

    @pl.when(jnp.logical_not(off_diag))
    def _():
        recv_p[0] = proj[tensor]

    def arrive_p(k, c):
        to_owner(k).wait_recv()
        return c

    lax.fori_loop(1, GROUPS, arrive_p, 0)
    summed = jnp.sum(recv_p[...].astype(jnp.float32), axis=0)
    squares = jnp.broadcast_to(jnp.sum(summed * summed, axis=1, keepdims=True), (ROWS, 128))
    ssq_own[...] = squares

    def to_tensor(k):
        return remote(
            ssq_own, recv_s.at[k], ss_send.at[k], ss_recv.at[k],
            {"tensor": (tensor + k) % GROUPS},
        )

    def start_tensor(k, c):
        to_tensor(k).start()
        return c

    lax.fori_loop(1, GROUPS, start_tensor, 0)
    recv_s[0] = squares

    def arrive_s(k, c):
        to_tensor(k).wait_recv()
        return c

    lax.fori_loop(1, GROUPS, arrive_s, 0)
    total = jnp.sum(recv_s[...], axis=0)[:, :1]
    inverse = lax.rsqrt(total * (1.0 / D) + 1e-05)
    out_ref[...] = (summed * inverse * gain_ref[...]).astype(jnp.bfloat16)

    def sent_a(i, c):
        for way in range(2):
            to_relay(way, i).wait_send()
            to_near(way, i, False).wait_send()
            to_near(way, i, True).wait_send()
        return c

    lax.fori_loop(0, half, sent_a, 0)

    def sent_plane(k, c):
        to_plane(k).wait_send()
        return c

    def sent_eight(k, c):
        to_y(k).wait_send()
        to_group(k).wait_send()
        to_owner(k).wait_send()
        to_tensor(k).wait_send()
        return c

    lax.fori_loop(1, PLANE, sent_plane, 0)
    lax.fori_loop(1, GROUPS, sent_eight, 0)

    @pl.when(off_diag)
    def _():
        to_owner(0).wait_send()


def body(queries, key_cache, value_cache, cached_len, block_slot, out_weight, norm_gain):
    vmem = pl.BlockSpec(memory_space=pltpu.VMEM)
    smem = pl.BlockSpec(memory_space=pltpu.SMEM)
    dma = pltpu.SemaphoreType.DMA
    bf16, f32 = jnp.bfloat16, jnp.float32
    n_ctx = REQS * PLANE
    weight_rows = out_weight.T
    gathered = pl.pallas_call(
        gather_kernel,
        out_shape=jax.ShapeDtypeStruct((n_ctx, ROWS, FEATS), bf16),
        in_specs=[vmem],
        out_specs=vmem,
        scratch_shapes=[dma, dma((PLANE,)), dma((REQS - 1, PLANE)), dma((n_ctx,))],
        compiler_params=pltpu.CompilerParams(collective_id=0, has_side_effects=True),
        name="gather_queries",
    )(queries)
    parts = pl.pallas_call(
        attention_kernel,
        out_shape=jax.ShapeDtypeStruct((REQS, SPAN, WIDE), bf16),
        in_specs=[smem, smem, vmem, vmem, vmem],
        out_specs=vmem,
        name="attention",
    )(block_slot, cached_len, gathered.reshape(n_ctx * ROWS, FEATS), key_cache, value_cache)
    return pl.pallas_call(
        finish_kernel,
        out_shape=jax.ShapeDtypeStruct((ROWS, FEATS), bf16),
        in_specs=[vmem] * 3,
        out_specs=vmem,
        scratch_shapes=[
            pltpu.VMEM((2, PLANE // 2, ROWS, WIDE), bf16),
            pltpu.VMEM((2, PLANE // 2, ROWS, WIDE), bf16),
            pltpu.VMEM((2, PLANE, ROWS, WIDE), bf16),
            pltpu.VMEM((PLANE, ROWS, WIDE), bf16),
            pltpu.VMEM((PLANE, ROWS, WIDE), bf16),
            pltpu.VMEM((YS, FEATS // YS, FEATS), bf16),
            pltpu.VMEM((ROWS, FEATS), bf16),
            pltpu.VMEM((GROUPS, ROWS, FEATS), bf16),
            pltpu.VMEM((GROUPS, ROWS, FEATS), bf16),
            pltpu.VMEM((GROUPS, ROWS, FEATS), bf16),
            pltpu.VMEM((ROWS, 128), f32),
            pltpu.VMEM((GROUPS, ROWS, 128), f32),
            dma((2, PLANE // 2)), dma((2, PLANE // 2)),
            dma((2, PLANE)), dma((2, PLANE)),
            dma((PLANE,)), dma((PLANE,)),
            dma((YS,)), dma((YS,)),
            dma((GROUPS,)), dma((GROUPS,)),
            dma((GROUPS,)), dma((GROUPS,)),
            dma((GROUPS,)), dma((GROUPS,)),
            dma,
        ],
        compiler_params=pltpu.CompilerParams(collective_id=1, has_side_effects=True),
        name="merge_project_norm",
    )(parts, weight_rows, norm_gain.reshape(1, FEATS))


def solution(mesh):
    in_specs = (
        P("ctx", "tensor"),
        P("ctx", None, "tensor"),
        P("ctx", None, "tensor"),
        P(),
        P(),
        P("tensor", "ctx"),
        P("tensor"),
    )
    out_specs = P("ctx", "tensor")
    return jax.shard_map(body, mesh=mesh, in_specs=in_specs, out_specs=out_specs, check_vma=False)
```

```python
import functools
import math

import jax
import jax.numpy as jnp
from jax import lax
from jax.experimental import pallas as pl
from jax.experimental.pallas import tpu as pltpu
from jax.sharding import PartitionSpec as P

HD = 96
REQS = 4
HEADS_DEV = 4
FEATS = 384
SPAN = 256
PLANE = 16
ROWS = 16
YS = 8
GROUPS = 8
D = 3072
NEG = -1e30
WIDE = FEATS + 128


def remote(src, dst, send, recv, device):
    return pltpu.make_async_remote_copy(
        src_ref=src,
        dst_ref=dst,
        send_sem=send,
        recv_sem=recv,
        device_id=device,
        device_id_type=pl.DeviceIdType.MESH,
    )


def signal(sem, device):
    pl.semaphore_signal(sem, inc=1, device_id=device, device_id_type=pl.DeviceIdType.MESH)


def gather_kernel(q_ref, out_ref, own_sem, send_plane, send_x, recv):
    me = lax.axis_index("ctx")
    x, j = me // PLANE, me % PLANE
    barrier = pltpu.get_barrier_semaphore()

    def greet(k, c):
        signal(barrier, {"ctx": x * PLANE + (j + k) % PLANE})
        return c

    lax.fori_loop(1, PLANE, greet, 0)
    for dx in range(1, REQS):
        signal(barrier, {"ctx": (x + dx) % REQS * PLANE + j})
    own = pltpu.make_async_copy(q_ref, out_ref.at[me], own_sem)
    own.start()
    pl.semaphore_wait(barrier, PLANE - 1 + REQS - 1)

    def to_plane(k):
        there = x * PLANE + (j + k) % PLANE
        return remote(q_ref, out_ref.at[me], send_plane.at[k], recv.at[me], {"ctx": there})

    def to_x(k, dx):
        block = x * PLANE + (j + PLANE - k) % PLANE
        there = (x + dx) % REQS * PLANE + j
        src = q_ref if isinstance(k, int) and k == 0 else out_ref.at[block]
        return remote(
            src, out_ref.at[block], send_x.at[dx - 1, k], recv.at[block], {"ctx": there}
        )

    def start_plane(k, c):
        to_plane(k).start()
        return c

    for dx in range(1, REQS):
        to_x(0, dx).start()
    lax.fori_loop(1, PLANE, start_plane, 0)

    def forward(k, c):
        block = x * PLANE + (j + PLANE - k) % PLANE
        pltpu.make_async_copy(out_ref.at[block], out_ref.at[block], recv.at[block]).wait()
        for dx in range(1, REQS):
            to_x(k, dx).start()
        return c

    lax.fori_loop(1, PLANE, forward, 0)

    def arrive(k, c):
        for dx in range(1, REQS):
            block = (x + dx) % REQS * PLANE + (j + PLANE - k) % PLANE
            pltpu.make_async_copy(out_ref.at[block], out_ref.at[block], recv.at[block]).wait()
        return c

    lax.fori_loop(0, PLANE, arrive, 0)

    def sent(k, c):
        to_plane(k).wait_send()
        for dx in range(1, REQS):
            to_x(k, dx).wait_send()
        return c

    lax.fori_loop(1, PLANE, sent, 0)
    for dx in range(1, REQS):
        to_x(0, dx).wait_send()
    own.wait()


def split_parts(lse):
    lane = lax.broadcasted_iota(jnp.int32, lse.shape, 1)
    high = lse.astype(jnp.bfloat16).astype(jnp.float32)
    rest = lse - high
    mid = rest.astype(jnp.bfloat16).astype(jnp.float32)
    low = rest - mid
    part = lane % 4
    picked = jnp.where(part == 0, high, jnp.where(part == 1, mid, jnp.where(part == 2, low, 0.0)))
    return jnp.where(lane < 4 * HEADS_DEV, picked, 0.0).astype(jnp.bfloat16)


def attend(slot_id, s, table_ref, len_ref, q_ref, k_ref, v_ref):
    block_rows = k_ref.shape[1]
    scale = 1.0 / math.sqrt(HD)
    request = jnp.int32(-1)
    reach = jnp.int32(-(1 << 28))
    for r in range(REQS):
        for b in range(table_ref.shape[1]):
            hit = table_ref[r, b] == slot_id
            request = jnp.where(hit, r, request)
            reach = jnp.where(hit, len_ref[r] - b * block_rows, reach)
    diff = (
        lax.broadcasted_iota(jnp.int32, (SPAN, block_rows), 1)
        - lax.broadcasted_iota(jnp.int32, (SPAN, block_rows), 0)
    )
    visible = diff <= reach
    query = q_ref[:SPAN, :]
    for r in range(1, REQS):
        query = jnp.where(request == r, q_ref[r * SPAN : (r + 1) * SPAN, :], query)
    tiles = [jnp.zeros((SPAN, 128), jnp.float32) for _ in range(FEATS // 128)]
    lane = lax.broadcasted_iota(jnp.int32, (SPAN, 128), 1)
    lse = jnp.full((SPAN, 128), NEG, jnp.float32)
    for h in range(HEADS_DEV):
        first, last = h * HD // 128, (h * HD + HD + 127) // 128
        lo, hi = first * 128, last * 128
        col = lo + lax.broadcasted_iota(jnp.int32, (SPAN, hi - lo), 1)
        mine = (col >= h * HD) & (col < h * HD + HD)
        part = query[:, lo:hi]
        part = jnp.where(mine, part, jnp.zeros_like(part))
        scores = lax.dot_general(
            part, k_ref[s, :, lo:hi], (((1,), (1,)), ((), ())),
            preferred_element_type=jnp.float32,
        ) * scale
        scores = jnp.where(visible, scores, NEG)
        top = jnp.max(scores, axis=1, keepdims=True)
        weights = jnp.where(visible, jnp.exp(scores - top), 0.0)
        total = jnp.sum(weights, axis=1, keepdims=True)
        mixed = jnp.dot(
            weights.astype(jnp.bfloat16), v_ref[s, :, lo:hi],
            preferred_element_type=jnp.float32,
        )
        some = total > 0.0
        safe = jnp.where(some, total, 1.0)
        mixed = jnp.where(mine, mixed * (1.0 / safe), 0.0)
        for t in range(first, last):
            tiles[t] = tiles[t] + mixed[:, t * 128 - lo : t * 128 - lo + 128]
        level = jnp.where(some, top + jnp.log(safe), NEG)
        lse = jnp.where(lane // 4 == h, level, lse)
    return request, tiles, lse


def merge_slots(one, two, part_ref):
    lane = lax.broadcasted_iota(jnp.int32, (SPAN, 128), 1)
    held = jnp.where(one[0] == two[0], one[2], NEG)
    best = jnp.maximum(held, two[2])
    keep, take = jnp.exp(held - best), jnp.exp(two[2] - best)
    mass = keep + take
    keep, take = keep / mass, take / mass
    level = best + jnp.log(mass)
    for t in range(FEATS // 128):
        col = t * 128 + lane
        k_b = jnp.zeros((SPAN, 128), jnp.float32)
        t_b = jnp.zeros((SPAN, 128), jnp.float32)
        for h in range(HEADS_DEV):
            if h * HD < t * 128 + 128 and h * HD + HD > t * 128:
                mine = (col >= h * HD) & (col < h * HD + HD)
                k_b = jnp.where(mine, keep[:, 4 * h : 4 * h + 1], k_b)
                t_b = jnp.where(mine, take[:, 4 * h : 4 * h + 1], t_b)
        merged = one[1][t] * k_b + two[1][t] * t_b
        for r in range(REQS):
            picked = jnp.where(two[0] == r, merged, jnp.where(one[0] == r, one[1][t], 0.0))
            part_ref[r, :, t * 128 : t * 128 + 128] = picked.astype(jnp.bfloat16)
    for r in range(REQS):
        picked = jnp.where(two[0] == r, level, jnp.where(one[0] == r, one[2], NEG))
        part_ref[r, :, FEATS:] = split_parts(picked)


def spread(columns, width):
    row = lax.broadcasted_iota(jnp.int32, (128, columns), 0)
    col = lax.broadcasted_iota(jnp.int32, (128, columns), 1)
    hit = (row // 4 == col // width) & (row < 4 * HEADS_DEV)
    return jnp.where(hit, 1.0, 0.0).astype(jnp.bfloat16)


def finish_kernel(
    table_ref, len_ref, q_ref, k_ref, v_ref, w_ref, gain_ref, out_ref,
    part_ref, relay_in, relay_out, recv_a, comb, recv_b, w_all, attn_own, attn_all, proj, recv_p, ssq_own, recv_s,
    sr_send, sr_recv, sa_send, sa_recv, sb_send, sb_recv, sw_send, sw_recv, sg_send, sg_recv,
    sp_send, sp_recv, ss_send, ss_recv, diag_sem,
):
    me = lax.axis_index("ctx")
    tensor = lax.axis_index("tensor")
    x, j = me // PLANE, me % PLANE
    group, y = me // YS, me % YS
    barrier = pltpu.get_barrier_semaphore()
    off_diag = group != tensor

    def greet_plane(k, c):
        signal(barrier, {"ctx": x * PLANE + (j + k) % PLANE})
        return c

    def greet_eight(k, c):
        signal(barrier, {"ctx": (group + k) % GROUPS * YS + y})
        signal(barrier, {"tensor": (tensor + k) % GROUPS})
        signal(barrier, {"tensor": (group + GROUPS - k) % GROUPS, "ctx": tensor * YS + y})
        return c

    lax.fori_loop(1, PLANE, greet_plane, 0)
    lax.fori_loop(1, GROUPS, greet_eight, 0)

    @pl.when(off_diag)
    def _():
        signal(barrier, {"tensor": group, "ctx": tensor * YS + y})

    slots = k_ref.shape[0]
    one = attend(me * slots, 0, table_ref, len_ref, q_ref, k_ref, v_ref)
    pl.semaphore_wait(barrier, PLANE - 1 + 3 * (GROUPS - 1) + off_diag.astype(jnp.int32))

    def to_y(k):
        return remote(
            w_ref, w_all.at[y], sw_send.at[k], sw_recv.at[k], {"ctx": group * YS + (y + k) % YS}
        )

    def start_y(k, c):
        to_y(k).start()
        return c

    lax.fori_loop(1, YS, start_y, 0)
    own_w = pltpu.make_async_copy(w_ref, w_all.at[y], diag_sem)
    own_w.start()

    two = attend(me * slots + 1, 1, table_ref, len_ref, q_ref, k_ref, v_ref)
    merge_slots(one, two, part_ref)

    half = PLANE // 2
    toward = ((x + 1) % REQS, (x + REQS - 1) % REQS)

    def rows_of(k):
        return pl.ds(pl.multiple_of((j + k) % PLANE * ROWS, ROWS), ROWS)

    def to_relay(way, i):
        return remote(
            part_ref.at[(x + 2) % REQS, rows_of(2 * i + way)], relay_in.at[way, i],
            sr_send.at[way, i], sr_recv.at[way, i], {"ctx": toward[way] * PLANE + j},
        )

    def to_near(way, i, relayed):
        k = 2 * i + (way if relayed else 1 - way)
        src = relay_out.at[way, i] if relayed else part_ref.at[toward[way], rows_of(k)]
        return remote(
            src, recv_a.at[way, k], sa_send.at[way, k], sa_recv.at[way, k],
            {"ctx": toward[way] * PLANE + j},
        )

    def start_relays(t, c):
        for way in range(2):
            to_relay(way, (t + 1) % half).start()
        return c

    def start_near(t, c):
        for way in range(2):
            to_near(way, (t + 1) % half, False).start()
        return c

    lax.fori_loop(0, half, start_relays, 0)
    lax.fori_loop(0, half, start_near, 0)

    to_heads = spread(FEATS, HD)
    to_lanes = spread(128, 4)

    def level_of(parts, pick):
        return jnp.dot(parts, pick, preferred_element_type=jnp.float32)

    def to_plane(k):
        there = x * PLANE + (j + k) % PLANE
        return remote(comb.at[k], recv_b.at[k], sb_send.at[k], sb_recv.at[k], {"ctx": there})

    def combine(blocks):
        parts = [b[:, FEATS:] for b in blocks]
        wide = [level_of(p, to_heads) for p in parts]
        best = functools.reduce(jnp.maximum, wide)
        factors = [jnp.exp(w - best) for w in wide]
        mass = sum(factors)
        mixed = sum(b[:, :FEATS].astype(jnp.float32) * f for b, f in zip(blocks, factors))
        narrow = [level_of(p, to_lanes) for p in parts]
        top = functools.reduce(jnp.maximum, narrow)
        level = top + jnp.log(sum(jnp.exp(n - top) for n in narrow))
        return (mixed / mass).astype(jnp.bfloat16), split_parts(level)

    def relay(t, c):
        i = (t + 1) % half
        for way in range(2):
            to_relay(way, i).wait_recv()
        merged = [
            combine([relay_in[way, i], part_ref[toward[way], rows_of(2 * i + way), :]])
            for way in range(2)
        ]
        for way in range(2):
            relay_out[way, i, :, :FEATS] = merged[way][0]
            relay_out[way, i, :, FEATS:] = merged[way][1]
        for way in range(2):
            to_near(way, i, True).start()
        return c

    lax.fori_loop(0, half, relay, 0)

    def owned(i):
        for way in range(2):
            to_near(way, i, False).wait_recv()
            to_near(way, i, True).wait_recv()
        return [
            combine([part_ref[x, rows_of(k), :], recv_a[0, k], recv_a[1, k]])
            for k in (2 * i, 2 * i + 1)
        ]

    def reduce_x(i, c):
        merged = owned(i)
        for at in range(2):
            comb[2 * i + at, :, :FEATS] = merged[at][0]
            comb[2 * i + at, :, FEATS:] = merged[at][1]
        for at in range(2):
            to_plane(2 * i + at).start()
        return c

    lax.fori_loop(1, half, reduce_x, 0)
    merged = owned(0)
    comb[1, :, :FEATS] = merged[1][0]
    comb[1, :, FEATS:] = merged[1][1]
    to_plane(1).start()
    recv_b[0, :, :FEATS] = merged[0][0]
    recv_b[0, :, FEATS:] = merged[0][1]

    def arrive_b(k, c):
        to_plane(k).wait_recv()
        return c

    lax.fori_loop(1, PLANE, arrive_b, 0)
    levels = level_of(recv_b[:, :, FEATS:].reshape(PLANE * ROWS, 128), to_heads)
    levels = levels.reshape(PLANE, ROWS, FEATS)
    best = jnp.max(levels, axis=0)
    factors = jnp.exp(levels - best[None])
    mass = jnp.sum(factors, axis=0)
    mixed = jnp.sum(recv_b[:, :, :FEATS].astype(jnp.float32) * factors, axis=0)
    attn = (mixed / mass).astype(jnp.bfloat16)
    attn_own[...] = attn

    def to_group(k):
        return remote(
            attn_own, attn_all.at[group], sg_send.at[k], sg_recv.at[k],
            {"ctx": (group + k) % GROUPS * YS + y},
        )

    def start_group(k, c):
        to_group(k).start()
        return c

    lax.fori_loop(1, GROUPS, start_group, 0)
    attn_all[group] = attn
    own_w.wait()

    def arrive_g(k, c):
        to_y(k).wait_recv()
        to_group(k).wait_recv()
        return c

    lax.fori_loop(1, GROUPS, arrive_g, 0)
    partial = lax.dot_general(
        attn_all[...].reshape(GROUPS * ROWS, FEATS), w_all[...].reshape(FEATS, FEATS),
        (((1,), (1,)), ((), ())), preferred_element_type=jnp.float32,
    )
    proj[...] = partial.astype(jnp.bfloat16).reshape(GROUPS, ROWS, FEATS)

    def to_owner(k):
        there = (tensor + k) % GROUPS
        return remote(
            proj.at[there], recv_p.at[k], sp_send.at[k], sp_recv.at[k],
            {"tensor": group, "ctx": there * YS + y},
        )

    def start_owner(k, c):
        to_owner(k).start()
        return c

    lax.fori_loop(1, GROUPS, start_owner, 0)

    @pl.when(off_diag)
    def _():
        to_owner(0).start()
        to_owner(0).wait_recv()

    @pl.when(jnp.logical_not(off_diag))
    def _():
        recv_p[0] = proj[tensor]

    def arrive_p(k, c):
        to_owner(k).wait_recv()
        return c

    lax.fori_loop(1, GROUPS, arrive_p, 0)
    summed = jnp.sum(recv_p[...].astype(jnp.float32), axis=0)
    squares = jnp.broadcast_to(jnp.sum(summed * summed, axis=1, keepdims=True), (ROWS, 128))
    ssq_own[...] = squares

    def to_tensor(k):
        return remote(
            ssq_own, recv_s.at[k], ss_send.at[k], ss_recv.at[k],
            {"tensor": (tensor + k) % GROUPS},
        )

    def start_tensor(k, c):
        to_tensor(k).start()
        return c

    lax.fori_loop(1, GROUPS, start_tensor, 0)
    recv_s[0] = squares

    def arrive_s(k, c):
        to_tensor(k).wait_recv()
        return c

    lax.fori_loop(1, GROUPS, arrive_s, 0)
    total = jnp.sum(recv_s[...], axis=0)[:, :1]
    inverse = lax.rsqrt(total * (1.0 / D) + 1e-05)
    out_ref[...] = (summed * inverse * gain_ref[...]).astype(jnp.bfloat16)

    def sent_a(i, c):
        for way in range(2):
            to_relay(way, i).wait_send()
            to_near(way, i, False).wait_send()
            to_near(way, i, True).wait_send()
        return c

    lax.fori_loop(0, half, sent_a, 0)

    def sent_plane(k, c):
        to_plane(k).wait_send()
        return c

    def sent_eight(k, c):
        to_y(k).wait_send()
        to_group(k).wait_send()
        to_owner(k).wait_send()
        to_tensor(k).wait_send()
        return c

    lax.fori_loop(1, PLANE, sent_plane, 0)
    lax.fori_loop(1, GROUPS, sent_eight, 0)

    @pl.when(off_diag)
    def _():
        to_owner(0).wait_send()


def body(queries, key_cache, value_cache, cached_len, block_slot, out_weight, norm_gain):
    vmem = pl.BlockSpec(memory_space=pltpu.VMEM)
    smem = pl.BlockSpec(memory_space=pltpu.SMEM)
    dma = pltpu.SemaphoreType.DMA
    bf16, f32 = jnp.bfloat16, jnp.float32
    n_ctx = REQS * PLANE
    weight_rows = out_weight.T
    gathered = pl.pallas_call(
        gather_kernel,
        out_shape=jax.ShapeDtypeStruct((n_ctx, ROWS, FEATS), bf16),
        in_specs=[vmem],
        out_specs=vmem,
        scratch_shapes=[dma, dma((PLANE,)), dma((REQS - 1, PLANE)), dma((n_ctx,))],
        compiler_params=pltpu.CompilerParams(collective_id=0, has_side_effects=True),
        name="gather_queries",
    )(queries)
    return pl.pallas_call(
        finish_kernel,
        out_shape=jax.ShapeDtypeStruct((ROWS, FEATS), bf16),
        in_specs=[smem] * 2 + [vmem] * 5,
        out_specs=vmem,
        scratch_shapes=[
            pltpu.VMEM((REQS, SPAN, WIDE), bf16),
            pltpu.VMEM((2, PLANE // 2, ROWS, WIDE), bf16),
            pltpu.VMEM((2, PLANE // 2, ROWS, WIDE), bf16),
            pltpu.VMEM((2, PLANE, ROWS, WIDE), bf16),
            pltpu.VMEM((PLANE, ROWS, WIDE), bf16),
            pltpu.VMEM((PLANE, ROWS, WIDE), bf16),
            pltpu.VMEM((YS, FEATS // YS, FEATS), bf16),
            pltpu.VMEM((ROWS, FEATS), bf16),
            pltpu.VMEM((GROUPS, ROWS, FEATS), bf16),
            pltpu.VMEM((GROUPS, ROWS, FEATS), bf16),
            pltpu.VMEM((GROUPS, ROWS, FEATS), bf16),
            pltpu.VMEM((ROWS, 128), f32),
            pltpu.VMEM((GROUPS, ROWS, 128), f32),
            dma((2, PLANE // 2)), dma((2, PLANE // 2)),
            dma((2, PLANE)), dma((2, PLANE)),
            dma((PLANE,)), dma((PLANE,)),
            dma((YS,)), dma((YS,)),
            dma((GROUPS,)), dma((GROUPS,)),
            dma((GROUPS,)), dma((GROUPS,)),
            dma((GROUPS,)), dma((GROUPS,)),
            dma,
        ],
        compiler_params=pltpu.CompilerParams(collective_id=1, has_side_effects=True),
        name="attend_merge_project_norm",
    )(
        block_slot, cached_len, gathered.reshape(n_ctx * ROWS, FEATS), key_cache, value_cache,
        weight_rows, norm_gain.reshape(1, FEATS),
    )


def solution(mesh):
    in_specs = (
        P("ctx", "tensor"),
        P("ctx", None, "tensor"),
        P("ctx", None, "tensor"),
        P(),
        P(),
        P("tensor", "ctx"),
        P("tensor"),
    )
    out_specs = P("ctx", "tensor")
    return jax.shard_map(body, mesh=mesh, in_specs=in_specs, out_specs=out_specs, check_vma=False)
```

```python
import functools
import math

import jax
import jax.numpy as jnp
from jax import lax
from jax.experimental import pallas as pl
from jax.experimental.pallas import tpu as pltpu
from jax.sharding import PartitionSpec as P

HD = 96
REQS = 4
HEADS_DEV = 4
FEATS = 384
SPAN = 256
PLANE = 16
ROWS = 16
YS = 8
GROUPS = 8
D = 3072
NEG = -1e30
WIDE = FEATS + 128


def remote(src, dst, send, recv, device):
    return pltpu.make_async_remote_copy(
        src_ref=src,
        dst_ref=dst,
        send_sem=send,
        recv_sem=recv,
        device_id=device,
        device_id_type=pl.DeviceIdType.MESH,
    )


def signal(sem, device):
    pl.semaphore_signal(sem, inc=1, device_id=device, device_id_type=pl.DeviceIdType.MESH)


def gather_kernel(q_ref, out_ref, own_sem, send_plane, send_x, recv):
    me = lax.axis_index("ctx")
    x, j = me // PLANE, me % PLANE
    barrier = pltpu.get_barrier_semaphore()

    def greet(k, c):
        signal(barrier, {"ctx": x * PLANE + (j + k) % PLANE})
        return c

    lax.fori_loop(1, PLANE, greet, 0)
    for dx in range(1, REQS):
        signal(barrier, {"ctx": (x + dx) % REQS * PLANE + j})
    own = pltpu.make_async_copy(q_ref, out_ref.at[me], own_sem)
    own.start()
    pl.semaphore_wait(barrier, PLANE - 1 + REQS - 1)

    def to_plane(k):
        there = x * PLANE + (j + k) % PLANE
        return remote(q_ref, out_ref.at[me], send_plane.at[k], recv.at[me], {"ctx": there})

    def to_x(k, dx):
        block = x * PLANE + (j + PLANE - k) % PLANE
        there = (x + dx) % REQS * PLANE + j
        src = q_ref if isinstance(k, int) and k == 0 else out_ref.at[block]
        return remote(
            src, out_ref.at[block], send_x.at[dx - 1, k], recv.at[block], {"ctx": there}
        )

    def start_plane(k, c):
        to_plane(k).start()
        return c

    for dx in range(1, REQS):
        to_x(0, dx).start()
    lax.fori_loop(1, PLANE, start_plane, 0)

    def forward(k, c):
        block = x * PLANE + (j + PLANE - k) % PLANE
        pltpu.make_async_copy(out_ref.at[block], out_ref.at[block], recv.at[block]).wait()
        for dx in range(1, REQS):
            to_x(k, dx).start()
        return c

    lax.fori_loop(1, PLANE, forward, 0)

    def arrive(k, c):
        for dx in range(1, REQS):
            block = (x + dx) % REQS * PLANE + (j + PLANE - k) % PLANE
            pltpu.make_async_copy(out_ref.at[block], out_ref.at[block], recv.at[block]).wait()
        return c

    lax.fori_loop(0, PLANE, arrive, 0)

    def sent(k, c):
        to_plane(k).wait_send()
        for dx in range(1, REQS):
            to_x(k, dx).wait_send()
        return c

    lax.fori_loop(1, PLANE, sent, 0)
    for dx in range(1, REQS):
        to_x(0, dx).wait_send()
    own.wait()


def split_parts(lse):
    lane = lax.broadcasted_iota(jnp.int32, lse.shape, 1)
    high = lse.astype(jnp.bfloat16).astype(jnp.float32)
    rest = lse - high
    mid = rest.astype(jnp.bfloat16).astype(jnp.float32)
    low = rest - mid
    part = lane % 4
    picked = jnp.where(part == 0, high, jnp.where(part == 1, mid, jnp.where(part == 2, low, 0.0)))
    return jnp.where(lane < 4 * HEADS_DEV, picked, 0.0).astype(jnp.bfloat16)


def attend(slot_id, s, table_ref, len_ref, q_ref, k_ref, v_ref):
    block_rows = k_ref.shape[1]
    scale = 1.0 / math.sqrt(HD)
    request = jnp.int32(-1)
    reach = jnp.int32(-(1 << 28))
    for r in range(REQS):
        for b in range(table_ref.shape[1]):
            hit = table_ref[r, b] == slot_id
            request = jnp.where(hit, r, request)
            reach = jnp.where(hit, len_ref[r] - b * block_rows, reach)
    diff = (
        lax.broadcasted_iota(jnp.int32, (SPAN, block_rows), 1)
        - lax.broadcasted_iota(jnp.int32, (SPAN, block_rows), 0)
    )
    visible = diff <= reach
    query = q_ref[:SPAN, :]
    for r in range(1, REQS):
        query = jnp.where(request == r, q_ref[r * SPAN : (r + 1) * SPAN, :], query)
    tiles = [jnp.zeros((SPAN, 128), jnp.float32) for _ in range(FEATS // 128)]
    lane = lax.broadcasted_iota(jnp.int32, (SPAN, 128), 1)
    lse = jnp.full((SPAN, 128), NEG, jnp.float32)
    for h in range(HEADS_DEV):
        first, last = h * HD // 128, (h * HD + HD + 127) // 128
        lo, hi = first * 128, last * 128
        col = lo + lax.broadcasted_iota(jnp.int32, (SPAN, hi - lo), 1)
        mine = (col >= h * HD) & (col < h * HD + HD)
        part = query[:, lo:hi]
        part = jnp.where(mine, part, jnp.zeros_like(part))
        scores = lax.dot_general(
            part, k_ref[s, :, lo:hi], (((1,), (1,)), ((), ())),
            preferred_element_type=jnp.float32,
        ) * scale
        scores = jnp.where(visible, scores, NEG)
        top = jnp.max(scores, axis=1, keepdims=True)
        weights = jnp.where(visible, jnp.exp(scores - top), 0.0)
        total = jnp.sum(weights, axis=1, keepdims=True)
        mixed = jnp.dot(
            weights.astype(jnp.bfloat16), v_ref[s, :, lo:hi],
            preferred_element_type=jnp.float32,
        )
        some = total > 0.0
        safe = jnp.where(some, total, 1.0)
        mixed = jnp.where(mine, mixed * (1.0 / safe), 0.0)
        for t in range(first, last):
            tiles[t] = tiles[t] + mixed[:, t * 128 - lo : t * 128 - lo + 128]
        level = jnp.where(some, top + jnp.log(safe), NEG)
        lse = jnp.where(lane // 4 == h, level, lse)
    return request, tiles, lse


def merge_slots(one, two, part_ref):
    lane = lax.broadcasted_iota(jnp.int32, (SPAN, 128), 1)
    held = jnp.where(one[0] == two[0], one[2], NEG)
    best = jnp.maximum(held, two[2])
    keep, take = jnp.exp(held - best), jnp.exp(two[2] - best)
    mass = keep + take
    keep, take = keep / mass, take / mass
    level = best + jnp.log(mass)
    for t in range(FEATS // 128):
        col = t * 128 + lane
        k_b = jnp.zeros((SPAN, 128), jnp.float32)
        t_b = jnp.zeros((SPAN, 128), jnp.float32)
        for h in range(HEADS_DEV):
            if h * HD < t * 128 + 128 and h * HD + HD > t * 128:
                mine = (col >= h * HD) & (col < h * HD + HD)
                k_b = jnp.where(mine, keep[:, 4 * h : 4 * h + 1], k_b)
                t_b = jnp.where(mine, take[:, 4 * h : 4 * h + 1], t_b)
        merged = one[1][t] * k_b + two[1][t] * t_b
        for r in range(REQS):
            picked = jnp.where(two[0] == r, merged, jnp.where(one[0] == r, one[1][t], 0.0))
            part_ref[r, :, t * 128 : t * 128 + 128] = picked.astype(jnp.bfloat16)
    for r in range(REQS):
        picked = jnp.where(two[0] == r, level, jnp.where(one[0] == r, one[2], NEG))
        part_ref[r, :, FEATS:] = split_parts(picked)


def spread(columns, width):
    row = lax.broadcasted_iota(jnp.int32, (128, columns), 0)
    col = lax.broadcasted_iota(jnp.int32, (128, columns), 1)
    hit = (row // 4 == col // width) & (row < 4 * HEADS_DEV)
    return jnp.where(hit, 1.0, 0.0).astype(jnp.bfloat16)


def finish_kernel(
    table_ref, len_ref, q_ref, k_ref, v_ref, w_ref, gain_ref, out_ref,
    part_ref, recv_a, comb, recv_b, w_all, attn_own, attn_all, proj, recv_p, ssq_own, recv_s,
    sa_send, sa_recv, sb_send, sb_recv, sw_send, sw_recv, sg_send, sg_recv,
    sp_send, sp_recv, ss_send, ss_recv, diag_sem,
):
    me = lax.axis_index("ctx")
    tensor = lax.axis_index("tensor")
    x, j = me // PLANE, me % PLANE
    group, y = me // YS, me % YS
    barrier = pltpu.get_barrier_semaphore()
    off_diag = group != tensor

    def greet_plane(k, c):
        signal(barrier, {"ctx": x * PLANE + (j + k) % PLANE})
        return c

    def greet_eight(k, c):
        signal(barrier, {"ctx": (group + k) % GROUPS * YS + y})
        signal(barrier, {"tensor": (tensor + k) % GROUPS})
        signal(barrier, {"tensor": (group + GROUPS - k) % GROUPS, "ctx": tensor * YS + y})
        return c

    lax.fori_loop(1, PLANE, greet_plane, 0)
    lax.fori_loop(1, GROUPS, greet_eight, 0)

    @pl.when(off_diag)
    def _():
        signal(barrier, {"tensor": group, "ctx": tensor * YS + y})

    slots = k_ref.shape[0]
    one = attend(me * slots, 0, table_ref, len_ref, q_ref, k_ref, v_ref)
    pl.semaphore_wait(barrier, PLANE - 1 + 3 * (GROUPS - 1) + off_diag.astype(jnp.int32))

    def to_y(k):
        return remote(
            w_ref, w_all.at[y], sw_send.at[k], sw_recv.at[k], {"ctx": group * YS + (y + k) % YS}
        )

    def start_y(k, c):
        to_y(k).start()
        return c

    lax.fori_loop(1, YS, start_y, 0)
    own_w = pltpu.make_async_copy(w_ref, w_all.at[y], diag_sem)
    own_w.start()

    two = attend(me * slots + 1, 1, table_ref, len_ref, q_ref, k_ref, v_ref)
    merge_slots(one, two, part_ref)

    half = PLANE // 2

    def rows_of(k):
        return pl.ds(pl.multiple_of((j + k) % PLANE * ROWS, ROWS), ROWS)

    def to_x(dx, k):
        there = (x + dx) % REQS
        return remote(
            part_ref.at[there, rows_of(k)], recv_a.at[dx - 1, k],
            sa_send.at[dx - 1, k], sa_recv.at[dx - 1, k], {"ctx": there * PLANE + j},
        )

    def start_x(t, c):
        i = (t + 1) % half
        for k in (2 * i, 2 * i + 1):
            for dx in (2, 1, 3):
                to_x(dx, k).start()
        return c

    lax.fori_loop(0, half, start_x, 0)

    to_heads = spread(FEATS, HD)
    to_lanes = spread(128, 4)

    def level_of(parts, pick):
        return jnp.dot(parts, pick, preferred_element_type=jnp.float32)

    def to_plane(k):
        there = x * PLANE + (j + k) % PLANE
        return remote(comb.at[k], recv_b.at[k], sb_send.at[k], sb_recv.at[k], {"ctx": there})

    def combine(blocks):
        parts = [b[:, FEATS:] for b in blocks]
        wide = [level_of(p, to_heads) for p in parts]
        best = functools.reduce(jnp.maximum, wide)
        factors = [jnp.exp(w - best) for w in wide]
        mass = sum(factors)
        mixed = sum(b[:, :FEATS].astype(jnp.float32) * f for b, f in zip(blocks, factors))
        narrow = [level_of(p, to_lanes) for p in parts]
        top = functools.reduce(jnp.maximum, narrow)
        level = top + jnp.log(sum(jnp.exp(n - top) for n in narrow))
        return (mixed / mass).astype(jnp.bfloat16), split_parts(level)

    def owned(i):
        for k in (2 * i, 2 * i + 1):
            for dx in range(1, REQS):
                to_x(dx, k).wait_recv()
        return [
            combine([part_ref[x, rows_of(k), :]] + [recv_a[at, k] for at in range(REQS - 1)])
            for k in (2 * i, 2 * i + 1)
        ]

    def reduce_x(i, c):
        merged = owned(i)
        for at in range(2):
            comb[2 * i + at, :, :FEATS] = merged[at][0]
            comb[2 * i + at, :, FEATS:] = merged[at][1]
        for at in range(2):
            to_plane(2 * i + at).start()
        return c

    lax.fori_loop(1, half, reduce_x, 0)
    merged = owned(0)
    comb[1, :, :FEATS] = merged[1][0]
    comb[1, :, FEATS:] = merged[1][1]
    to_plane(1).start()
    recv_b[0, :, :FEATS] = merged[0][0]
    recv_b[0, :, FEATS:] = merged[0][1]

    def arrive_b(k, c):
        to_plane(k).wait_recv()
        return c

    lax.fori_loop(1, PLANE, arrive_b, 0)
    levels = level_of(recv_b[:, :, FEATS:].reshape(PLANE * ROWS, 128), to_heads)
    levels = levels.reshape(PLANE, ROWS, FEATS)
    best = jnp.max(levels, axis=0)
    factors = jnp.exp(levels - best[None])
    mass = jnp.sum(factors, axis=0)
    mixed = jnp.sum(recv_b[:, :, :FEATS].astype(jnp.float32) * factors, axis=0)
    attn = (mixed / mass).astype(jnp.bfloat16)
    attn_own[...] = attn

    def to_group(k):
        return remote(
            attn_own, attn_all.at[group], sg_send.at[k], sg_recv.at[k],
            {"ctx": (group + k) % GROUPS * YS + y},
        )

    def start_group(k, c):
        to_group(k).start()
        return c

    lax.fori_loop(1, GROUPS, start_group, 0)
    attn_all[group] = attn
    own_w.wait()

    def arrive_g(k, c):
        to_y(k).wait_recv()
        to_group(k).wait_recv()
        return c

    lax.fori_loop(1, GROUPS, arrive_g, 0)
    partial = lax.dot_general(
        attn_all[...].reshape(GROUPS * ROWS, FEATS), w_all[...].reshape(FEATS, FEATS),
        (((1,), (1,)), ((), ())), preferred_element_type=jnp.float32,
    )
    proj[...] = partial.astype(jnp.bfloat16).reshape(GROUPS, ROWS, FEATS)

    def to_owner(k):
        there = (tensor + k) % GROUPS
        return remote(
            proj.at[there], recv_p.at[k], sp_send.at[k], sp_recv.at[k],
            {"tensor": group, "ctx": there * YS + y},
        )

    def start_owner(k, c):
        to_owner(k).start()
        return c

    lax.fori_loop(1, GROUPS, start_owner, 0)

    @pl.when(off_diag)
    def _():
        to_owner(0).start()
        to_owner(0).wait_recv()

    @pl.when(jnp.logical_not(off_diag))
    def _():
        recv_p[0] = proj[tensor]

    def arrive_p(k, c):
        to_owner(k).wait_recv()
        return c

    lax.fori_loop(1, GROUPS, arrive_p, 0)
    summed = jnp.sum(recv_p[...].astype(jnp.float32), axis=0)
    squares = jnp.broadcast_to(jnp.sum(summed * summed, axis=1, keepdims=True), (ROWS, 128))
    ssq_own[...] = squares

    def to_tensor(k):
        return remote(
            ssq_own, recv_s.at[k], ss_send.at[k], ss_recv.at[k],
            {"tensor": (tensor + k) % GROUPS},
        )

    def start_tensor(k, c):
        to_tensor(k).start()
        return c

    lax.fori_loop(1, GROUPS, start_tensor, 0)
    recv_s[0] = squares

    def arrive_s(k, c):
        to_tensor(k).wait_recv()
        return c

    lax.fori_loop(1, GROUPS, arrive_s, 0)
    total = jnp.sum(recv_s[...], axis=0)[:, :1]
    inverse = lax.rsqrt(total * (1.0 / D) + 1e-05)
    out_ref[...] = (summed * inverse * gain_ref[...]).astype(jnp.bfloat16)

    def sent_a(k, c):
        for dx in range(1, REQS):
            to_x(dx, k).wait_send()
        return c

    lax.fori_loop(0, PLANE, sent_a, 0)

    def sent_plane(k, c):
        to_plane(k).wait_send()
        return c

    def sent_eight(k, c):
        to_y(k).wait_send()
        to_group(k).wait_send()
        to_owner(k).wait_send()
        to_tensor(k).wait_send()
        return c

    lax.fori_loop(1, PLANE, sent_plane, 0)
    lax.fori_loop(1, GROUPS, sent_eight, 0)

    @pl.when(off_diag)
    def _():
        to_owner(0).wait_send()


def body(queries, key_cache, value_cache, cached_len, block_slot, out_weight, norm_gain):
    vmem = pl.BlockSpec(memory_space=pltpu.VMEM)
    smem = pl.BlockSpec(memory_space=pltpu.SMEM)
    dma = pltpu.SemaphoreType.DMA
    bf16, f32 = jnp.bfloat16, jnp.float32
    n_ctx = REQS * PLANE
    weight_rows = out_weight.T
    gathered = pl.pallas_call(
        gather_kernel,
        out_shape=jax.ShapeDtypeStruct((n_ctx, ROWS, FEATS), bf16),
        in_specs=[vmem],
        out_specs=vmem,
        scratch_shapes=[dma, dma((PLANE,)), dma((REQS - 1, PLANE)), dma((n_ctx,))],
        compiler_params=pltpu.CompilerParams(collective_id=0, has_side_effects=True),
        name="gather_queries",
    )(queries)
    return pl.pallas_call(
        finish_kernel,
        out_shape=jax.ShapeDtypeStruct((ROWS, FEATS), bf16),
        in_specs=[smem] * 2 + [vmem] * 5,
        out_specs=vmem,
        scratch_shapes=[
            pltpu.VMEM((REQS, SPAN, WIDE), bf16),
            pltpu.VMEM((REQS - 1, PLANE, ROWS, WIDE), bf16),
            pltpu.VMEM((PLANE, ROWS, WIDE), bf16),
            pltpu.VMEM((PLANE, ROWS, WIDE), bf16),
            pltpu.VMEM((YS, FEATS // YS, FEATS), bf16),
            pltpu.VMEM((ROWS, FEATS), bf16),
            pltpu.VMEM((GROUPS, ROWS, FEATS), bf16),
            pltpu.VMEM((GROUPS, ROWS, FEATS), bf16),
            pltpu.VMEM((GROUPS, ROWS, FEATS), bf16),
            pltpu.VMEM((ROWS, 128), f32),
            pltpu.VMEM((GROUPS, ROWS, 128), f32),
            dma((REQS - 1, PLANE)), dma((REQS - 1, PLANE)),
            dma((PLANE,)), dma((PLANE,)),
            dma((YS,)), dma((YS,)),
            dma((GROUPS,)), dma((GROUPS,)),
            dma((GROUPS,)), dma((GROUPS,)),
            dma((GROUPS,)), dma((GROUPS,)),
            dma,
        ],
        compiler_params=pltpu.CompilerParams(collective_id=1, has_side_effects=True),
        name="attend_merge_project_norm",
    )(
        block_slot, cached_len, gathered.reshape(n_ctx * ROWS, FEATS), key_cache, value_cache,
        weight_rows, norm_gain.reshape(1, FEATS),
    )


def solution(mesh):
    in_specs = (
        P("ctx", "tensor"),
        P("ctx", None, "tensor"),
        P("ctx", None, "tensor"),
        P(),
        P(),
        P("tensor", "ctx"),
        P("tensor"),
    )
    out_specs = P("ctx", "tensor")
    return jax.shard_map(body, mesh=mesh, in_specs=in_specs, out_specs=out_specs, check_vma=False)
```
